128 devices in a mesh: row: 4 (over y), col: 32 (over x, z, core).
Axes of the slice: x: 4, y: 4, z: 4, core: 2. Of those that a mesh axis runs over, the one named last changes fastest.
Arguments:
- frontal: bfloat16 [16384, 49152], P('row', 'col')
- sample_cols: bfloat16 [49152, 64], P(('col', 'row')), may hold values from -6 to 6
- leaf_first: int32 [256], replicated, may hold values from 0 to 16352, as said below
- leaf_owner: int32 [256], replicated, may hold values from 0 to 31, as said below
- skeleton: int32 [256, 16], replicated, may hold values from 0 to 16383, as said below
Outputs:
- owner_samples: float32 [256, 8192], P('row', 'col')
- interp: float32 [64, 8192], P('row', 'col')
- worst: float32 [1], replicated
The draws below stay inside these ranges and needn't reach their ends.
Inputs may be any that keep to these rules, and one draw needn't show every extreme that they name: `leaf_first`: leaves are consecutive and ascending; the first leaf of row group g starts at g * 4096; each row group has 64 leaves whose sizes are 1 to 5 times 32, in 16 runs of four consecutive leaves of together 256 rows. `leaf_owner`: each run of four leaves is owned by at most two devices of the group; the leaves one device owns in its group hold at most 256 rows and number at most 4; in every row group some device reaches both. Each leaf's skeleton rows are 16 distinct rows of that leaf, ascending.
All inputs are finite; a program needn't handle non-finite values.
Results may differ from the reference program's by a relative error of at most 0.0003.
Values may be sent and summed in bfloat16 or wider, within the bound.
A program may use at most 64 MiB of HBM per device.

```python
import jax
import jax.numpy as jnp
from jax import lax

MATRIX_ORDER = 49152
SAMPLES = 64
SKELETON = 16
ROWS_OWNED = 128
CAPACITY = 256
GROUP_ROWS = 4096
WINDOW_ROWS = 16384
LEAVES = 256
N_ROW = 4
N_COL = 32


def leaf_tables(key):
    unit = ROWS_OWNED // 4
    pairs = N_COL // 2
    key_cut, key_side, key_owner, key_skel = jax.random.split(jax.random.fold_in(key, 7), 4)
    cut_scores = jax.random.randint(key_cut, (N_ROW, pairs, 7), 0, 1 << 20) * 8 + jnp.arange(7, dtype=jnp.int32)
    picked = jnp.sort(jnp.argsort(cut_scores, axis=-1)[..., :3].astype(jnp.int32) + 1, axis=-1)
    zeros = jnp.zeros((N_ROW, pairs, 1), jnp.int32)
    bounds = jnp.concatenate([zeros, picked, zeros + 8], axis=-1)
    units = bounds[..., 1:] - bounds[..., :-1]
    sides = jax.random.randint(key_side, (N_ROW, pairs, 4), 0, 2)
    first_pair = (jnp.arange(pairs, dtype=jnp.int32) == 0)[None, :, None]
    sides = jnp.where(first_pair, 0, sides)
    owner_scores = jax.random.randint(key_owner, (N_ROW, N_COL), 0, 1 << 20) * N_COL + jnp.arange(N_COL, dtype=jnp.int32)
    order = jnp.argsort(owner_scores, axis=-1).astype(jnp.int32)
    first_owner = order[:, 0::2]
    second_owner = order[:, 1::2]
    owner = jnp.where(sides == 0, first_owner[..., None], second_owner[..., None]).reshape(LEAVES)
    sizes = (units * unit).reshape(N_ROW, 2 * N_COL)
    starts = jnp.cumsum(sizes, axis=1) - sizes + (jnp.arange(N_ROW, dtype=jnp.int32) * GROUP_ROWS)[:, None]
    starts = starts.reshape(LEAVES).astype(jnp.int32)
    flat_sizes = sizes.reshape(LEAVES)
    top = 5 * unit
    skel_scores = jax.random.randint(key_skel, (LEAVES, top), 0, 1 << 20) * top + jnp.arange(top, dtype=jnp.int32)
    inside = jnp.arange(top, dtype=jnp.int32)[None, :] < flat_sizes[:, None]
    skel_scores = jnp.where(inside, skel_scores, (1 << 20) * top + top)
    chosen = jnp.sort(jnp.argsort(skel_scores, axis=-1)[:, :SKELETON].astype(jnp.int32), axis=-1)
    return (starts, owner.astype(jnp.int32), (chosen + starts[:, None]).astype(jnp.int32))


def draw_leaf_first(key, part):
    return leaf_tables(key)[0]


def draw_leaf_owner(key, part):
    return leaf_tables(key)[1]


def draw_skeleton(key, part):
    return leaf_tables(key)[2]


def draw_frontal(key, part):
    shape = (WINDOW_ROWS, MATRIX_ORDER)
    noise = jax.random.normal(key, shape, jnp.float32)
    base = MATRIX_ORDER ** (-0.5)
    rows = jnp.arange(WINDOW_ROWS, dtype=jnp.float32)[:, None]
    cols = jnp.arange(WINDOW_ROWS, dtype=jnp.float32)[None, :]
    near = base + 0.1 * jnp.exp(-jnp.abs(rows - cols) / ROWS_OWNED)
    left = noise[:, :WINDOW_ROWS] * near
    right = noise[:, WINDOW_ROWS:] * base
    return jnp.concatenate([left, right], axis=1).astype(jnp.bfloat16)


def block_levels(key, extent, pieces, least, top_value):
    def one(axis_at, parts):
        steps = jax.random.uniform(jax.random.fold_in(jax.random.fold_in(key, 6), axis_at), (parts,), jnp.float32, least / len(pieces), top_value / len(pieces))
        return jnp.repeat(jnp.exp(steps), extent[axis_at] // parts).reshape((-1,) + (1,) * (len(extent) - axis_at - 1))

    gain = one(*pieces[0])
    for cut in pieces[1:]:
        gain = gain * one(*cut)
    return gain


def normal_values(own_key, extent, width, bound, pieces=(), kind=jnp.bfloat16):
    values = jax.random.normal(own_key, extent, jnp.float32) * width
    if len(pieces) > 0:
        values = block_levels(own_key, extent, pieces, -0.22, 0.18) * values
    return jnp.clip(values, min=-bound, max=bound).astype(kind)


def setup_inputs(seed: int = 0) -> dict:
    key_of = jax.random.split(jax.random.key(seed), 6)
    return {
        "frontal": draw_frontal(jax.random.fold_in(key_of[5], 71), 0),
        "sample_cols": normal_values(key_of[1], (MATRIX_ORDER, SAMPLES), 1.0, 6.0, ((0, 128),)),
        "leaf_first": draw_leaf_first(jax.random.fold_in(key_of[5], 71), 0),
        "leaf_owner": draw_leaf_owner(jax.random.fold_in(key_of[5], 71), 0),
        "skeleton": draw_skeleton(jax.random.fold_in(key_of[5], 71), 0),
    }


def leaf_index(values, leaf_first):
    return lax.optimization_barrier(jnp.sum((leaf_first[None, :] <= values[:, None]).astype(jnp.int32), axis=1)) - 1

def reference(frontal, sample_cols, leaf_first, leaf_owner, skeleton):
    highest = lax.Precision.HIGHEST
    rows = jnp.arange(WINDOW_ROWS, dtype=jnp.int32)
    row_leaf = leaf_index(rows, leaf_first)
    near_cols = sample_cols[:WINDOW_ROWS]

    def block(carry, index):
        start = (index * GROUP_ROWS).astype(jnp.int32)
        part = lax.dynamic_slice_in_dim(frontal, start, GROUP_ROWS, 0)
        leaves_here = lax.dynamic_slice_in_dim(row_leaf, start, GROUP_ROWS, 0)
        full = jnp.dot(part.astype(jnp.float32), sample_cols.astype(jnp.float32), preferred_element_type=jnp.float32)
        same = leaves_here[:, None] == row_leaf[None, :]
        kept = jnp.where(same, part[:, :WINDOW_ROWS], jnp.zeros((), frontal.dtype))
        diag = jnp.dot(kept.astype(jnp.float32), near_cols.astype(jnp.float32), preferred_element_type=jnp.float32)
        return (carry, full - diag)
    _, blocks = lax.scan(block, jnp.zeros((), jnp.float32), jnp.arange(N_ROW, dtype=jnp.int32))
    samples = blocks.reshape(WINDOW_ROWS, SAMPLES)
    ends = jnp.concatenate([leaf_first[1:], jnp.full((1,), WINDOW_ROWS, jnp.int32)])
    sizes = ends - leaf_first
    per_group = 2 * N_COL
    own_hot = (leaf_owner[:, None] == jnp.arange(N_COL, dtype=jnp.int32)[None, :]).astype(jnp.int32)
    weighted = (own_hot * sizes[:, None]).reshape(N_ROW, per_group, N_COL)
    before = (jnp.cumsum(weighted, axis=1) - weighted).reshape(LEAVES, N_COL)
    offset = lax.optimization_barrier(jnp.sum(before * own_hot, axis=1))
    slot = leaf_owner[row_leaf] * CAPACITY + offset[row_leaf] + rows - leaf_first[row_leaf]
    row_group = rows // GROUP_ROWS
    picked = samples[skeleton]
    gram = jnp.einsum('lkp,ljp->lkj', picked, picked, precision=highest)
    eye = jnp.broadcast_to(jnp.eye(SKELETON, dtype=jnp.float32), gram.shape)
    ginv = jnp.linalg.solve(gram, eye)
    picked_rows = picked[row_leaf]
    proj = jnp.einsum('ikp,ip->ik', picked_rows, samples, precision=highest)
    coeff = jnp.einsum('ij,ijk->ik', proj, ginv[row_leaf], precision=highest)
    rebuilt = jnp.einsum('ik,ikp->ip', coeff, picked_rows, precision=highest)
    resid = samples - rebuilt
    err = jax.ops.segment_sum(lax.optimization_barrier(jnp.sum(resid * resid, axis=1)), row_leaf, LEAVES)
    norm = jax.ops.segment_sum(lax.optimization_barrier(jnp.sum(samples * samples, axis=1)), row_leaf, LEAVES)
    ratio = jnp.sqrt(err) / jnp.sqrt(norm + 1e-06)
    worst = jnp.max(ratio).reshape(1)
    holder = jnp.zeros((N_ROW, N_COL * CAPACITY, SAMPLES), jnp.float32).at[row_group, slot].set(samples)
    owner_samples = jnp.transpose(holder, (0, 2, 1)).reshape(N_ROW * SAMPLES, N_COL * CAPACITY)
    cholder = jnp.zeros((N_ROW, N_COL * CAPACITY, SKELETON), jnp.float32).at[row_group, slot].set(coeff)
    interp = jnp.transpose(cholder, (0, 2, 1)).reshape(N_ROW * SKELETON, N_COL * CAPACITY)
    return (owner_samples, interp, worst)
```

```python
import functools
import math

import jax
import jax.numpy as jnp
from jax import lax
from jax.experimental import pallas as pl
from jax.experimental.pallas import tpu as pltpu
from jax.sharding import PartitionSpec as P

UNIT = 32
RUN = 256
LANES = 128
LEAF_MOST = 4
F32 = jnp.float32
I32 = jnp.int32
MESH = pl.DeviceIdType.MESH
HI = lax.Precision.HIGHEST
NT = (((1,), (1,)), ((), ()))
NN = (((1,), (0,)), ((), ()))


def dot(a, b, dims, precision=None):
    return lax.dot_general(a, b, dims, precision=precision, preferred_element_type=F32)


def iota(shape, axis):
    return lax.broadcasted_iota(I32, shape, axis)


def kernel(
    cfg,
    frontal,
    piece,
    lf_s,
    lf_v,
    lo_v,
    sk_v,
    samples_out,
    interp_out,
    worst_out,
    a_v,
    pt,
    part,
    cx,
    s1,
    ph1,
    rot,
    pk,
    ph2,
    s3,
    mt,
    table_v,
    table_s,
    w0,
    w1,
    w2,
    w3,
    a_sem,
    t_sem,
    pc_send,
    pc_recv,
    cx_send,
    cx_recv,
    p1_send,
    p1_recv,
    p2_send,
    p2_recv,
    a2_send,
    a2_recv,
    m_send,
    m_recv,
):
    (rows, width, p_all, ny, nx, leaves_group, skel, cap, chunk) = cfg
    n_chunk = rows // chunk
    per_run = chunk // RUN
    tiles = rows // LANES
    half_p = p_all // 2
    sl = half_p // nx
    owners = 2 * nx
    per_owner = cap // UNIT
    depth = width // ny

    g = lax.axis_index("row")
    me = lax.axis_index("col")
    core = lax.rem(me, 2)
    z = lax.rem(me // 2, nx)
    x = me // (2 * nx)
    q = jnp.where(core == 0, x, z)
    b = jnp.where(core == 0, z, x)

    def col_of(xx, zz, cc):
        return (xx * nx + zz) * 2 + cc

    def ring_a(pos):
        return col_of(jnp.where(core == 0, pos, x), jnp.where(core == 0, z, pos), core)

    def ring_b(pos):
        return col_of(jnp.where(core == 0, x, pos), jnp.where(core == 0, pos, z), core)

    def remote(src, dst, send, recv, row, col):
        return pltpu.make_async_remote_copy(
            src_ref=src,
            dst_ref=dst,
            send_sem=send,
            recv_sem=recv,
            device_id=(row, col),
            device_id_type=MESH,
        )

    def load(i):
        at = pl.ds(pl.multiple_of(i * chunk, chunk), chunk)
        return pltpu.make_async_copy(frontal.at[at], a_v.at[at], a_sem.at[i])

    for i in range(n_chunk):
        load(i).start()

    barrier = pltpu.get_barrier_semaphore()
    count = 0
    for d in range(1, ny):
        pl.semaphore_signal(barrier, inc=1, device_id=(lax.rem(g + d, ny), me), device_id_type=MESH)
        count += 1
    j_x = x * 2 + core
    for d in range(1, owners):
        j = lax.rem(j_x + d, owners)
        to = col_of(j // 2, z, lax.rem(j, 2))
        pl.semaphore_signal(barrier, inc=1, device_id=(g, to), device_id_type=MESH)
        count += 1
    for d in range(1, nx):
        for cc in range(2):
            to = col_of(x, lax.rem(z + d, nx), cc)
            pl.semaphore_signal(barrier, inc=1, device_id=(g, to), device_id_type=MESH)
            count += 1
    pl.semaphore_wait(barrier, count)

    def piece_copy(d):
        at = pl.ds(pl.multiple_of(g * depth, LANES), depth)
        return remote(piece, pt.at[:, at], pc_send.at[d - 1], pc_recv.at[d - 1], lax.rem(g + d, ny), me)

    for d in range(1, ny):
        piece_copy(d).start()
    pt[:, pl.ds(pl.multiple_of(g * depth, LANES), depth)] = piece[...]

    nl = leaves_group
    lane = iota((1, LANES), 1)

    def group_lanes(v):
        out = None
        for gi in range(ny):
            part_v = v if gi == 0 else pltpu.roll(v, v.shape[1] - gi * nl, axis=1)
            part_v = part_v[:, :LANES]
            out = part_v if out is None else jnp.where(g == gi, part_v, out)
        return out

    first = group_lanes(lf_v[...])
    owner = group_lanes(lo_v[...])
    real = lane < nl
    owner = jnp.where(real, owner, -1)
    fu = jnp.where(real, (first - g * rows) // UNIT, 0)
    nxt = pltpu.roll(fu, LANES - 1, axis=1)
    nxt = jnp.where(lane == nl - 1, rows // UNIT, nxt)
    su = jnp.where(real, nxt - fu, 0)
    owner_t = jnp.transpose(jnp.broadcast_to(owner, (LANES, LANES)))
    fu_t = jnp.transpose(jnp.broadcast_to(fu, (LANES, LANES)))
    su_t = jnp.transpose(jnp.broadcast_to(su, (LANES, LANES)))
    li = iota((LANES, LANES), 0)
    lj = iota((LANES, LANES), 1)
    same = owner == owner_t
    before = same & (li < lj)
    after = same & (lj < li)
    off = jnp.sum(jnp.where(before, su_t, 0), axis=0, keepdims=True)
    rank = jnp.sum(jnp.where(before, 1, 0), axis=0, keepdims=True)
    off_t = jnp.sum(jnp.where(after, su, 0), axis=1, keepdims=True)
    rank_t = jnp.sum(jnp.where(after, 1, 0), axis=1, keepdims=True)
    slots_all = owners * nx * per_owner
    dst = iota((1, slots_all), 1)
    d_owner = dst // per_owner
    d_su = lax.rem(dst, per_owner)
    o1 = owner_t[:, :1]
    f1 = fu_t[:, :1]
    u1 = su_t[:, :1]
    hit = (o1 == d_owner) & (off_t <= d_su) & (d_su < off_t + u1)
    src = jnp.sum(jnp.where(hit, f1 + d_su - off_t + 1, 0), axis=0, keepdims=True) - 1
    per_tile = LANES // UNIT
    turn = lax.rem(d_su - src + 8 * per_tile * rows, per_tile)
    entry = jnp.where(src >= 0, turn * tiles + src // per_tile, per_tile * tiles)
    table_v[...] = entry
    to_smem = pltpu.make_async_copy(table_v, table_s, t_sem)
    to_smem.start()

    slot = iota((1, cap), 1)
    slot_u = slot // UNIT
    mine_t = (o1 == me) & (off_t <= slot_u) & (slot_u < off_t + u1)
    slot_rank = jnp.sum(jnp.where(mine_t, rank_t + 1, 0), axis=0, keepdims=True) - 1
    sk = group_lanes(sk_v[...])
    sk_slot = sk - first + off * UNIT + 1
    cols = []
    for k in range(LEAF_MOST):
        pick_k = (owner == me) & (rank == k)
        cols.append(jnp.sum(jnp.where(pick_k, sk_slot, 0), axis=1, keepdims=True))
    sk_col = jnp.concatenate(cols, axis=0)
    hot = jnp.where(sk_col == slot + 1, 1.0, 0.0).astype(F32)
    ki = LEAF_MOST * skel
    row_k = iota((ki, 1), 0) // skel

    for d in range(1, ny):
        piece_copy(d).wait_recv()

    def mask_run(t):
        run = g * (rows // RUN) + t
        blocks = width // RUN

        @pl.when(run // blocks == me)
        def _():
            r0 = pl.multiple_of(t * RUN, RUN)
            c0 = pl.multiple_of(lax.rem(run, blocks) * RUN, RUN)
            ri = iota((RUN, RUN), 0) + run * RUN
            ci = iota((RUN, RUN), 1) + run * RUN
            rl = jnp.zeros((RUN, RUN), I32)
            cl = jnp.zeros((RUN, RUN), I32)
            for k in range(1, 4):
                edge = lf_s[run * 4 + k]
                rl = rl + jnp.where(ri >= edge, 1, 0)
                cl = cl + jnp.where(ci >= edge, 1, 0)
            block = a_v[pl.ds(r0, RUN), pl.ds(c0, RUN)].astype(F32)
            a_v[pl.ds(r0, RUN), pl.ds(c0, RUN)] = jnp.where(rl == cl, 0.0, block).astype(jnp.bfloat16)

    sibling = col_of(x, z, 1 - core)

    def core_copy(i):
        at = pl.ds(pl.multiple_of(i * chunk, chunk), chunk)
        theirs = pl.ds(pl.multiple_of((1 - core) * half_p, half_p), half_p)
        return remote(part.at[theirs, at], cx.at[:, at], cx_send.at[i], cx_recv.at[i], g, sibling)

    def first_copy(i, d):
        to = lax.rem(q + d, nx)
        at = pl.ds(pl.multiple_of(i * chunk, chunk), chunk)
        rows_at = pl.ds(pl.multiple_of(to * sl, sl), sl)
        s = i * (nx - 1) + d - 1
        return remote(s1.at[rows_at, at], ph1.at[d - 1, :, at], p1_send.at[s], p1_recv.at[s], g, ring_a(to))

    def core_sum(i):
        at = pl.ds(pl.multiple_of(i * chunk, chunk), chunk)
        own = pl.ds(pl.multiple_of(core * half_p, half_p), half_p)
        core_copy(i).wait_recv()
        s1[:, at] = part[own, at] + cx[:, at]
        for d in range(1, nx):
            first_copy(i, d).start()

    def step(i, carry):
        load(i).wait()
        for t in range(per_run):
            mask_run(i * per_run + t)
        for t in range(per_run):
            at = pl.ds(pl.multiple_of(i * chunk + t * RUN, RUN), RUN)
            part[:, at] = dot(pt[...], a_v[at, :], NT)
        core_copy(i).start()

        @pl.when(i > 0)
        def _():
            core_sum(i - 1)

        return carry

    lax.fori_loop(0, n_chunk, step, 0)
    core_sum(n_chunk - 1)
    to_smem.wait()

    rot[per_tile * tiles] = jnp.zeros((sl, LANES), F32)

    def first_sum(i, carry):
        for d in range(1, nx):
            first_copy(i, d).wait_recv()
        own = pl.ds(pl.multiple_of(q * sl, sl), sl)
        for t in range(chunk // LANES):
            at = pl.ds(pl.multiple_of(i * chunk + t * LANES, LANES), LANES)
            v = s1[own, at]
            for d in range(1, nx):
                v = v + ph1[d - 1, :, at]
            tile = i * (chunk // LANES) + t
            rot[tile] = v
            for k in range(1, per_tile):
                rot[k * tiles + tile] = pltpu.roll(v, k * UNIT, axis=1)
        return carry

    lax.fori_loop(0, n_chunk, first_sum, 0)

    lane_u = iota((sl, LANES), 1) // UNIT

    def second_copy(d):
        to = lax.rem(b + d, nx)
        return remote(pk.at[d], ph2.at[d - 1], p2_send.at[d - 1], p2_recv.at[d - 1], g, ring_b(to))

    for d in [*range(1, nx), 0]:
        to = lax.rem(b + d, nx)

        def pack(j, carry, d=d, to=to):
            o = jnp.where(core == 0, col_of(j // 2, to, lax.rem(j, 2)), col_of(to, j // 2, lax.rem(j, 2)))
            for h in range(cap // LANES):
                base = o * per_owner + h * per_tile
                v = rot[table_s[0, base]]
                for k in range(1, per_tile):
                    v = jnp.where(lane_u == k, rot[table_s[0, base + k]], v)
                pk[d, :, pl.ds(pl.multiple_of(j * cap + h * LANES, LANES), LANES)] = v
            return carry

        lax.fori_loop(0, owners, pack, 0)
        if d > 0:
            second_copy(d).start()

    for d in range(1, nx):
        second_copy(d).wait_recv()
    total = pk[0]
    for d in range(1, nx):
        total = total + ph2[d - 1]
    s3[...] = total

    j_me = q * 2 + core
    slice_me = core * nx + q
    slice_rows = pl.ds(pl.multiple_of(slice_me * sl, sl), sl)

    def owner_copy(d):
        j = lax.rem(j_me + d, owners)
        to = jnp.where(core == 0, col_of(j // 2, z, lax.rem(j, 2)), col_of(x, j // 2, lax.rem(j, 2)))
        at = pl.ds(pl.multiple_of(j * cap, cap), cap)
        return remote(s3.at[:, at], mt.at[slice_rows, :], a2_send.at[d - 1], a2_recv.at[slice_me], g, to)

    def owner_wait(d):
        s = lax.rem(slice_me + d, owners)
        at = pl.ds(pl.multiple_of(s * sl, sl), sl)
        src_at = pl.ds(0, cap)
        return remote(s3.at[:, src_at], mt.at[at, :], a2_send.at[d - 1], a2_recv.at[s], g, sibling)

    for d in range(1, owners):
        owner_copy(d).start()
    mt[slice_rows, :] = s3[:, pl.ds(pl.multiple_of(j_me * cap, cap), cap)]
    for d in range(1, owners):
        owner_wait(d).wait_recv()

    m = mt[...]
    samples_out[...] = m
    pick = dot(hot, m, NT, HI)
    pick_t = dot(m, hot, NT, HI)
    rhs = dot(pick, m, NN, HI)
    gram = dot(pick, pick, NT, HI)
    col_k = iota((1, ki), 1) // skel
    in_block = row_k == col_k
    gram = jnp.where(in_block, gram, 0.0)
    folded = gram[:skel]
    for k in range(1, LEAF_MOST):
        folded = folded + gram[k * skel : (k + 1) * skel]
    here = jnp.concatenate(
        [jnp.broadcast_to(jnp.where(c[:1] > 0, 1, 0), (1, skel)) for c in cols], axis=1
    )
    eye_i = iota((skel, ki), 0)
    eye_r = lax.rem(iota((skel, ki), 1), skel)
    a = []
    for j in range(skel):
        v = None
        for k in range(LEAF_MOST):
            c = jnp.broadcast_to(folded[:, k * skel + j : k * skel + j + 1], (skel, ki))
            v = c if v is None else jnp.where(col_k == k, c, v)
        a.append(v + jnp.where((eye_i == j) & (here == 0), 1.0, 0.0))
    inv = jnp.where(eye_i == eye_r, 1.0, 0.0).astype(F32)
    for s in range(skel):
        col = a[s]
        rcp = 1.0 / col[s : s + 1]
        at_s = eye_i == s
        for j in range(s + 1, skel):
            t = a[j][s : s + 1] * rcp
            a[j] = jnp.where(at_s, t, a[j] - col * t)
        t = inv[s : s + 1] * rcp
        inv = jnp.where(at_s, t, inv - col * t)
    inv_all = jnp.where(in_block, jnp.concatenate([inv] * LEAF_MOST, axis=0), 0.0)
    rhs = jnp.where(row_k == slot_rank, rhs, 0.0)
    coeff = dot(inv_all, rhs, NN, HI)
    folded_c = coeff[:skel]
    for k in range(1, LEAF_MOST):
        folded_c = folded_c + coeff[k * skel : (k + 1) * skel]
    interp_out[...] = folded_c
    resid = m - dot(pick_t, coeff, NN, HI)
    err = jnp.sum(resid * resid, axis=0, keepdims=True)
    norm = jnp.sum(m * m, axis=0, keepdims=True)
    of_k = iota((8, 1), 0) == slot_rank
    err = jnp.sum(jnp.where(of_k, err, 0.0), axis=1, keepdims=True)
    norm = jnp.sum(jnp.where(of_k, norm, 0.0), axis=1, keepdims=True)
    ratio = jnp.sqrt(err) / jnp.sqrt(norm + 1e-06)
    w0[...] = jnp.broadcast_to(jnp.max(ratio, axis=0, keepdims=True), w0.shape)

    def m1(d):
        j = lax.rem(j_x + d, owners)
        return remote(w0, w1.at[d - 1], m_send.at[d - 1], m_recv.at[d - 1], g, col_of(j // 2, z, lax.rem(j, 2)))

    base2 = owners - 1
    base3 = base2 + nx - 1

    def m2(d):
        s = base2 + d - 1
        return remote(w2.at[0], w2.at[d], m_send.at[s], m_recv.at[s], g, col_of(x, lax.rem(z + d, nx), core))

    def m3(d):
        s = base3 + d - 1
        return remote(w3.at[0], w3.at[d], m_send.at[s], m_recv.at[s], lax.rem(g + d, ny), me)

    for d in range(1, owners):
        m1(d).start()
    for d in range(1, owners):
        m1(d).wait_recv()
    v = w0[...]
    for d in range(1, owners):
        v = jnp.maximum(v, w1[d - 1])
    w2[0] = v
    for d in range(1, nx):
        m2(d).start()
    for d in range(1, nx):
        m2(d).wait_recv()
    for d in range(1, nx):
        v = jnp.maximum(v, w2[d])
    w3[0] = v
    for d in range(1, ny):
        m3(d).start()
    for d in range(1, ny):
        m3(d).wait_recv()
    for d in range(1, ny):
        v = jnp.maximum(v, w3[d])
    worst_out[...] = v[:1]

    for d in range(1, ny):
        piece_copy(d).wait_send()
        m3(d).wait_send()

    def drain(i, carry):
        core_copy(i).wait_send()
        for d in range(1, nx):
            first_copy(i, d).wait_send()
        return carry

    lax.fori_loop(0, n_chunk, drain, 0)
    for d in range(1, nx):
        second_copy(d).wait_send()
        m2(d).wait_send()
    for d in range(1, owners):
        owner_copy(d).wait_send()
        m1(d).wait_send()


def local(frontal, sample_cols, leaf_first, leaf_owner, skeleton):
    rows, width = frontal.shape
    p_all = sample_cols.shape[1]
    leaves, skel = skeleton.shape
    ncol = lax.axis_size("col")
    ny = lax.axis_size("row")
    nx = math.isqrt(ncol // 2)
    cap = 2 * rows // ncol
    chunk = 512
    n_chunk = rows // chunk
    tiles = rows // LANES
    half_p = p_all // 2
    sl = half_p // nx
    owners = 2 * nx
    cfg = (rows, width, p_all, ny, nx, leaves // ny, skel, cap, chunk)
    slots_all = ncol * cap // UNIT
    vmem = pl.BlockSpec(memory_space=pltpu.VMEM)
    smem = pl.BlockSpec(memory_space=pltpu.SMEM)
    dma = pltpu.SemaphoreType.DMA
    n_m = owners - 1 + nx - 1 + ny - 1
    pad = ((0, 0), (0, max(0, LANES - leaves)))
    samples, interp, worst = pl.pallas_call(
        functools.partial(kernel, cfg),
        out_shape=(
            jax.ShapeDtypeStruct((p_all, cap), F32),
            jax.ShapeDtypeStruct((skel, cap), F32),
            jax.ShapeDtypeStruct((1, LANES), F32),
        ),
        in_specs=[pl.BlockSpec(memory_space=pl.ANY), vmem, smem, vmem, vmem, vmem],
        out_specs=(vmem, vmem, vmem),
        scratch_shapes=[
            pltpu.VMEM((rows, width), jnp.bfloat16),
            pltpu.VMEM((p_all, width), jnp.bfloat16),
            pltpu.VMEM((p_all, rows), F32),
            pltpu.VMEM((half_p, rows), F32),
            pltpu.VMEM((half_p, rows), F32),
            pltpu.VMEM((nx - 1, sl, rows), F32),
            pltpu.VMEM((4 * tiles + 1, sl, LANES), F32),
            pltpu.VMEM((nx, sl, owners * cap), F32),
            pltpu.VMEM((nx - 1, sl, owners * cap), F32),
            pltpu.VMEM((sl, owners * cap), F32),
            pltpu.VMEM((p_all, cap), F32),
            pltpu.VMEM((1, slots_all), I32),
            pltpu.SMEM((1, slots_all), I32),
            pltpu.VMEM((8, LANES), F32),
            pltpu.VMEM((owners - 1, 8, LANES), F32),
            pltpu.VMEM((nx, 8, LANES), F32),
            pltpu.VMEM((ny, 8, LANES), F32),
            dma((n_chunk,)),
            dma(()),
            dma((ny - 1,)),
            dma((ny - 1,)),
            dma((n_chunk,)),
            dma((n_chunk,)),
            dma((n_chunk * (nx - 1),)),
            dma((n_chunk * (nx - 1),)),
            dma((nx - 1,)),
            dma((nx - 1,)),
            dma((owners - 1,)),
            dma((owners,)),
            dma((n_m,)),
            dma((n_m,)),
        ],
        compiler_params=pltpu.CompilerParams(
            collective_id=0, has_side_effects=True, vmem_limit_bytes=60 << 20
        ),
        name="round",
    )(
        frontal,
        sample_cols.T,
        leaf_first,
        jnp.pad(leaf_first.reshape(1, leaves), pad),
        jnp.pad(leaf_owner.reshape(1, leaves), pad),
        jnp.pad(skeleton.T, pad),
    )
    return samples, interp, worst[0, :1]


def solution(mesh):
    return jax.shard_map(
        local,
        mesh=mesh,
        in_specs=(P("row", "col"), P(("col", "row"), None), P(), P(), P()),
        out_specs=(P("row", "col"), P("row", "col"), P()),
        check_vma=False,
    )
```

```python
import functools
import math

import jax
import jax.numpy as jnp
from jax import lax
from jax.experimental import pallas as pl
from jax.experimental.pallas import tpu as pltpu
from jax.sharding import PartitionSpec as P

UNIT = 32
RUN = 256
LANES = 128
LEAF_MOST = 4
F32 = jnp.float32
I32 = jnp.int32
MESH = pl.DeviceIdType.MESH
HI = lax.Precision.HIGHEST
NT = (((1,), (1,)), ((), ()))
NN = (((1,), (0,)), ((), ()))


def dot(a, b, dims, precision=None):
    return lax.dot_general(a, b, dims, precision=precision, preferred_element_type=F32)


def iota(shape, axis):
    return lax.broadcasted_iota(I32, shape, axis)


def out_kind(*shapes):
    return tuple(jax.ShapeDtypeStruct(s, F32) for s in shapes)


def kernel(
    cfg,
    frontal,
    piece,
    lf_h1,
    lf_h,
    lo_h,
    sk_h,
    samples_out,
    interp_out,
    worst_out,
    a_v,
    pt,
    lf_s,
    lf_v,
    lo_v,
    sk_v,
    part,
    cx,
    s1,
    ph1,
    rot,
    pk,
    rx,
    table_v,
    table_s,
    w0,
    w1,
    w2,
    w3,
    a_sem,
    l_sem,
    t_sem,
    near_sem,
    pc_send,
    pc_recv,
    cx_send,
    cx_recv,
    p1_send,
    p1_recv,
    o_send,
    o_recv,
    m_send,
    m_recv,
):
    (rows, width, p_all, ny, nx, leaves_group, skel, cap, chunk) = cfg
    n_chunk = rows // chunk
    per_run = chunk // RUN
    tiles = rows // LANES
    half_p = p_all // 2
    sl = half_p // nx
    owners = 2 * nx
    n_col = owners * nx
    per_owner = cap // UNIT
    depth = width // ny

    g = lax.axis_index("row")
    me = lax.axis_index("col")
    core = lax.rem(me, 2)
    z = lax.rem(me // 2, nx)
    x = me // (2 * nx)
    q = jnp.where(core == 0, x, z)
    j_x = x * 2 + core

    def col_of(xx, zz, cc):
        return (xx * nx + zz) * 2 + cc

    def ring_a(pos):
        return col_of(jnp.where(core == 0, pos, x), jnp.where(core == 0, z, pos), core)

    def remote(src, dst, send_at, recv_at, row, col):
        return pltpu.make_async_remote_copy(
            src_ref=src,
            dst_ref=dst,
            send_sem=send_at,
            recv_sem=recv_at,
            device_id=(row, col),
            device_id_type=MESH,
        )

    def signal(sem, row, col):
        pl.semaphore_signal(sem, inc=1, device_id=(row, col), device_id_type=MESH)

    barrier = pltpu.get_barrier_semaphore()
    count = 0
    for d in range(1, ny):
        signal(barrier, lax.rem(g + d, ny), me)
        count += 1
    for d in range(1, owners):
        j = lax.rem(j_x + d, owners)
        signal(barrier, g, col_of(j // 2, z, lax.rem(j, 2)))
        count += 1
    for d in range(1, nx):
        for cc in range(2):
            signal(barrier, g, col_of(x, lax.rem(z + d, nx), cc))
            count += 1

    def load(i):
        at = pl.ds(pl.multiple_of(i * chunk, chunk), chunk)
        return pltpu.make_async_copy(frontal.at[at], a_v.at[at], a_sem.at[i])

    own_at = pl.ds(pl.multiple_of(g * depth, LANES), depth)
    small = [
        pltpu.make_async_copy(piece, pt.at[:, own_at], l_sem.at[0]),
        pltpu.make_async_copy(lf_h1, lf_s, l_sem.at[1]),
        pltpu.make_async_copy(lf_h, lf_v, l_sem.at[2]),
        pltpu.make_async_copy(lo_h, lo_v, l_sem.at[3]),
        pltpu.make_async_copy(sk_h, sk_v, l_sem.at[4]),
    ]
    for c in small:
        c.start()
    for i in range(n_chunk):
        load(i).start()
    pl.semaphore_wait(barrier, count)

    drains = []

    def send(copy):
        copy().start()
        drains.append(lambda: copy().wait_send())

    def piece_copy(d):
        to = lax.rem(g + d, ny)
        return remote(piece, pt.at[:, own_at], pc_send.at[d - 1], pc_recv.at[d - 1], to, me)

    turns = sorted(range(1, ny), key=lambda d: min(d, ny - d))
    for d in turns:
        send(functools.partial(piece_copy, d))

    for d in range(1, nx):
        signal(near_sem, g, col_of(x, lax.rem(z + d, nx), core))
    for d in range(1, ny):
        signal(near_sem, lax.rem(g + d, ny), me)

    for c in small:
        c.wait()
    nl = leaves_group
    lane = iota((1, LANES), 1)

    def group_lanes(v):
        out = None
        for gi in range(ny):
            part_v = v if gi == 0 else pltpu.roll(v, v.shape[1] - gi * nl, axis=1)
            part_v = part_v[:, :LANES]
            out = part_v if out is None else jnp.where(g == gi, part_v, out)
        return out

    first = group_lanes(lf_v[...])
    owner = group_lanes(lo_v[...])
    real = lane < nl
    owner = jnp.where(real, owner, -1)
    fu = jnp.where(real, (first - g * rows) // UNIT, 0)
    nxt = pltpu.roll(fu, LANES - 1, axis=1)
    nxt = jnp.where(lane == nl - 1, rows // UNIT, nxt)
    su = jnp.where(real, nxt - fu, 0)
    owner_t = jnp.transpose(jnp.broadcast_to(owner, (LANES, LANES)))
    fu_t = jnp.transpose(jnp.broadcast_to(fu, (LANES, LANES)))
    su_t = jnp.transpose(jnp.broadcast_to(su, (LANES, LANES)))
    li = iota((LANES, LANES), 0)
    lj = iota((LANES, LANES), 1)
    same = owner == owner_t
    before = same & (li < lj)
    after = same & (lj < li)
    off = jnp.sum(jnp.where(before, su_t, 0), axis=0, keepdims=True)
    rank = jnp.sum(jnp.where(before, 1, 0), axis=0, keepdims=True)
    off_t = jnp.sum(jnp.where(after, su, 0), axis=1, keepdims=True)
    rank_t = jnp.sum(jnp.where(after, 1, 0), axis=1, keepdims=True)
    dst = iota((1, n_col * per_owner), 1)
    d_owner = dst // per_owner
    d_su = lax.rem(dst, per_owner)
    o1 = owner_t[:, :1]
    f1 = fu_t[:, :1]
    u1 = su_t[:, :1]
    hit = (o1 == d_owner) & (off_t <= d_su) & (d_su < off_t + u1)
    src = jnp.sum(jnp.where(hit, f1 + d_su - off_t + 1, 0), axis=0, keepdims=True) - 1
    per_tile = LANES // UNIT
    turn = lax.rem(d_su - src + 8 * per_tile * rows, per_tile)
    entry = jnp.where(src >= 0, turn * tiles + src // per_tile, per_tile * tiles)
    table_v[...] = entry
    to_smem = pltpu.make_async_copy(table_v, table_s, t_sem)
    to_smem.start()

    slot = iota((1, cap), 1)
    slot_u = slot // UNIT
    mine_t = (o1 == me) & (off_t <= slot_u) & (slot_u < off_t + u1)
    slot_rank = jnp.sum(jnp.where(mine_t, rank_t + 1, 0), axis=0, keepdims=True) - 1
    sk = group_lanes(sk_v[...])
    sk_slot = sk - first + off * UNIT + 1
    cols = []
    for k in range(LEAF_MOST):
        pick_k = (owner == me) & (rank == k)
        cols.append(jnp.sum(jnp.where(pick_k, sk_slot, 0), axis=1, keepdims=True))
    sk_col = jnp.concatenate(cols, axis=0)
    hot = jnp.where(sk_col == slot + 1, 1.0, 0.0).astype(F32)
    ki = LEAF_MOST * skel
    row_k = iota((ki, 1), 0) // skel

    def mask_run(t):
        run = g * (rows // RUN) + t
        blocks = width // RUN

        @pl.when(run // blocks == me)
        def _():
            r0 = pl.multiple_of(t * RUN, RUN)
            c0 = pl.multiple_of(lax.rem(run, blocks) * RUN, RUN)
            ri = iota((RUN, RUN), 0) + run * RUN
            ci = iota((RUN, RUN), 1) + run * RUN
            rl = jnp.zeros((RUN, RUN), I32)
            cl = jnp.zeros((RUN, RUN), I32)
            for k in range(1, 4):
                edge = lf_s[run * 4 + k]
                rl = rl + jnp.where(ri >= edge, 1, 0)
                cl = cl + jnp.where(ci >= edge, 1, 0)
            block = a_v[pl.ds(r0, RUN), pl.ds(c0, RUN)].astype(F32)
            a_v[pl.ds(r0, RUN), pl.ds(c0, RUN)] = jnp.where(rl == cl, 0.0, block).astype(jnp.bfloat16)

    def product(i, t, d):
        at = pl.ds(pl.multiple_of(i * chunk + t * RUN, RUN), RUN)
        k_at = pl.ds(pl.multiple_of(lax.rem(g + d, ny) * depth, LANES), depth)
        return at, dot(pt[:, k_at], a_v[at, k_at], NT)

    def own_step(i, carry):
        load(i).wait()
        for t in range(per_run):
            mask_run(i * per_run + t)
        for t in range(per_run):
            at, v = product(i, t, 0)
            part[:, at] = v
        return carry

    lax.fori_loop(0, n_chunk, own_step, 0)

    sibling = col_of(x, z, 1 - core)

    def core_copy(i):
        at = pl.ds(pl.multiple_of(i * chunk, chunk), chunk)
        theirs = pl.ds(pl.multiple_of((1 - core) * half_p, half_p), half_p)
        return remote(part.at[theirs, at], cx.at[:, at], cx_send.at[i], cx_recv.at[i], g, sibling)

    def add_step(i, carry, ds, last):
        for t in range(per_run):
            for d in ds:
                at, v = product(i, t, d)
                part[:, at] += v
        if last:
            core_copy(i).start()
        return carry

    for n, d in enumerate(turns):
        piece_copy(d).wait_recv()
        lax.fori_loop(0, n_chunk, functools.partial(add_step, ds=[ny - d], last=n == ny - 2), 0)

    def first_copy(i, d):
        to = lax.rem(q + d, nx)
        at = pl.ds(pl.multiple_of(i * chunk, chunk), chunk)
        rows_at = pl.ds(pl.multiple_of(to * sl, sl), sl)
        s = i * (nx - 1) + d - 1
        return remote(s1.at[rows_at, at], ph1.at[d - 1, :, at], p1_send.at[s], p1_recv.at[s], g, ring_a(to))

    def core_sum(i, carry):
        at = pl.ds(pl.multiple_of(i * chunk, chunk), chunk)
        own = pl.ds(pl.multiple_of(core * half_p, half_p), half_p)
        core_copy(i).wait_recv()
        s1[:, at] = part[own, at] + cx[:, at]
        for d in range(1, nx):
            first_copy(i, d).start()
        return carry

    def drain(i, carry):
        core_copy(i).wait_send()
        for d in range(1, nx):
            first_copy(i, d).wait_send()
        return carry

    lax.fori_loop(0, n_chunk, core_sum, 0)
    drains.append(lambda: lax.fori_loop(0, n_chunk, drain, 0))

    rot[per_tile * tiles] = jnp.zeros((sl, LANES), F32)

    def first_sum(i, carry):
        for d in range(1, nx):
            first_copy(i, d).wait_recv()
        own = pl.ds(pl.multiple_of(q * sl, sl), sl)
        for t in range(chunk // LANES):
            at = pl.ds(pl.multiple_of(i * chunk + t * LANES, LANES), LANES)
            v = s1[own, at]
            for d in range(1, nx):
                v = v + ph1[d - 1, :, at]
            tile = i * (chunk // LANES) + t
            rot[tile] = v
            for k in range(1, per_tile):
                rot[k * tiles + tile] = pltpu.roll(v, k * UNIT, axis=1)
        return carry

    lax.fori_loop(0, n_chunk, first_sum, 0)

    to_smem.wait()
    pl.semaphore_wait(near_sem, nx - 1 + ny - 1)
    lane_u = iota((sl, LANES), 1) // UNIT

    def owner_copy(k):
        to = lax.rem(me + k, n_col)
        return remote(pk.at[k], rx.at[me], o_send.at[k], o_recv.at[me], g, to)

    def owner_wait(k):
        frm = lax.rem(me + k, n_col)
        return remote(pk.at[k], rx.at[frm], o_send.at[k], o_recv.at[frm], g, frm)

    def block_of(o, h):
        base = o * per_owner + h * per_tile
        v = rot[table_s[0, base]]
        for k in range(1, per_tile):
            v = jnp.where(lane_u == k, rot[table_s[0, base + k]], v)
        return v

    def pack(k, carry):
        o = lax.rem(me + k, n_col)
        for h in range(cap // LANES):
            pk[k, :, h * LANES : (h + 1) * LANES] = block_of(o, h)
        owner_copy(k).start()
        return carry

    def owner_loop(do):
        def one(k, carry):
            do(k)
            return carry

        lax.fori_loop(1, n_col, one, 0)

    lax.fori_loop(1, n_col, pack, 0)
    for h in range(cap // LANES):
        rx[me, :, h * LANES : (h + 1) * LANES] = block_of(me, h)
    owner_loop(lambda k: owner_wait(k).wait_recv())
    drains.append(lambda: owner_loop(lambda k: owner_copy(k).wait_send()))

    def total(ids):
        v = rx[ids[0]]
        for s in ids[1:]:
            v = v + rx[s]
        return v

    m = jnp.concatenate(
        [total([col_of(a, b, 0) for b in range(nx)]) for a in range(nx)]
        + [total([col_of(b, a, 1) for b in range(nx)]) for a in range(nx)],
        axis=0,
    )

    samples_out[...] = m
    pick = dot(hot, m, NT, HI)
    pick_t = dot(m, hot, NT, HI)
    rhs = dot(pick, m, NN, HI)
    gram = dot(pick, pick, NT, HI)
    col_k = iota((1, ki), 1) // skel
    in_block = row_k == col_k
    gram = jnp.where(in_block, gram, 0.0)
    folded = gram[:skel]
    for k in range(1, LEAF_MOST):
        folded = folded + gram[k * skel : (k + 1) * skel]
    here = jnp.concatenate(
        [jnp.broadcast_to(jnp.where(c[:1] > 0, 1, 0), (1, skel)) for c in cols], axis=1
    )
    eye_i = iota((skel, ki), 0)
    eye_r = lax.rem(iota((skel, ki), 1), skel)
    a = []
    for j in range(skel):
        v = None
        for k in range(LEAF_MOST):
            c = jnp.broadcast_to(folded[:, k * skel + j : k * skel + j + 1], (skel, ki))
            v = c if v is None else jnp.where(col_k == k, c, v)
        a.append(v + jnp.where((eye_i == j) & (here == 0), 1.0, 0.0))
    inv = jnp.where(eye_i == eye_r, 1.0, 0.0).astype(F32)
    for s in range(skel):
        col = a[s]
        rcp = 1.0 / col[s : s + 1]
        at_s = eye_i == s
        for j in range(s + 1, skel):
            t = a[j][s : s + 1] * rcp
            a[j] = jnp.where(at_s, t, a[j] - col * t)
        t = inv[s : s + 1] * rcp
        inv = jnp.where(at_s, t, inv - col * t)
    inv_all = jnp.where(in_block, jnp.concatenate([inv] * LEAF_MOST, axis=0), 0.0)
    rhs = jnp.where(row_k == slot_rank, rhs, 0.0)
    coeff = dot(inv_all, rhs, NN, HI)
    resid = m - dot(pick_t, coeff, NN, HI)
    err = jnp.sum(resid * resid, axis=0, keepdims=True)
    norm = jnp.sum(m * m, axis=0, keepdims=True)
    of_k = iota((8, 1), 0) == slot_rank
    err = jnp.sum(jnp.where(of_k, err, 0.0), axis=1, keepdims=True)
    norm = jnp.sum(jnp.where(of_k, norm, 0.0), axis=1, keepdims=True)
    ratio = jnp.sqrt(err) / jnp.sqrt(norm + 1e-06)
    w0[...] = jnp.broadcast_to(jnp.max(ratio, axis=0, keepdims=True), w0.shape)

    def m1(d):
        j = lax.rem(j_x + d, owners)
        to = col_of(j // 2, z, lax.rem(j, 2))
        return remote(w0.at[:1], w1.at[d - 1, :1], m_send.at[d - 1], m_recv.at[d - 1], g, to)

    def m2(d):
        s = owners - 2 + d
        to_y = lax.rem(g + d // nx, ny)
        to = col_of(x, lax.rem(z + d % nx, nx), core)
        return remote(w2.at[:1], w3.at[d - 1, :1], m_send.at[s], m_recv.at[s], to_y, to)

    for d in range(1, owners):
        send(functools.partial(m1, d))
    folded_c = coeff[:skel]
    for k in range(1, LEAF_MOST):
        folded_c = folded_c + coeff[k * skel : (k + 1) * skel]
    interp_out[...] = folded_c
    for d in range(1, owners):
        m1(d).wait_recv()
    v = w0[:1]
    for d in range(1, owners):
        v = jnp.maximum(v, w1[d - 1, :1])
    w2[...] = jnp.broadcast_to(v, w2.shape)
    for d in range(1, nx * ny):
        send(functools.partial(m2, d))
    for f in drains:
        f()
    for d in range(1, nx * ny):
        m2(d).wait_recv()
    for d in range(1, nx * ny):
        v = jnp.maximum(v, w3[d - 1, :1])
    worst_out[...] = v


def finish(a_ref, b_ref, c_ref, a_out, b_out, c_out):
    a_out[...] = a_ref[...]
    b_out[...] = b_ref[...]
    c_out[...] = c_ref[:, :1]


def local(frontal, sample_cols, leaf_first, leaf_owner, skeleton):
    rows, width = frontal.shape
    p_all = sample_cols.shape[1]
    leaves, skel = skeleton.shape
    n_col = lax.axis_size("col")
    ny = lax.axis_size("row")
    nx = math.isqrt(n_col // 2)
    cap = 2 * rows // n_col
    chunk = 512
    n_chunk = rows // chunk
    tiles = rows // LANES
    half_p = p_all // 2
    sl = half_p // nx
    owners = 2 * nx
    cfg = (rows, width, p_all, ny, nx, leaves // ny, skel, cap, chunk)
    slots_all = n_col * cap // UNIT
    hbm = pl.BlockSpec(memory_space=pl.ANY)
    vmem = pl.BlockSpec(memory_space=pltpu.VMEM)
    dma = pltpu.SemaphoreType.DMA
    n_m = owners - 1 + nx * ny - 1
    pad = ((0, 0), (0, max(0, LANES - leaves)))
    wide = leaves + pad[1][1]
    results = pl.pallas_call(
        functools.partial(kernel, cfg),
        out_shape=out_kind((p_all, cap), (skel, cap), (1, LANES)),
        in_specs=[hbm] * 6,
        out_specs=(vmem, vmem, vmem),
        scratch_shapes=[
            pltpu.VMEM((rows, width), jnp.bfloat16),
            pltpu.VMEM((p_all, width), jnp.bfloat16),
            pltpu.SMEM((leaves,), I32),
            pltpu.VMEM((1, wide), I32),
            pltpu.VMEM((1, wide), I32),
            pltpu.VMEM((skel, wide), I32),
            pltpu.VMEM((p_all, rows), F32),
            pltpu.VMEM((half_p, rows), F32),
            pltpu.VMEM((half_p, rows), F32),
            pltpu.VMEM((nx - 1, sl, rows), F32),
            pltpu.VMEM((4 * tiles + 1, sl, LANES), F32),
            pltpu.VMEM((n_col, sl, cap), F32),
            pltpu.VMEM((n_col, sl, cap), F32),
            pltpu.VMEM((1, slots_all), I32),
            pltpu.SMEM((1, slots_all), I32),
            pltpu.VMEM((8, LANES), F32),
            pltpu.VMEM((owners - 1, 8, LANES), F32),
            pltpu.VMEM((8, LANES), F32),
            pltpu.VMEM((nx * ny - 1, 8, LANES), F32),
            dma((n_chunk,)),
            dma((5,)),
            dma(()),
            pltpu.SemaphoreType.REGULAR,
            dma((ny - 1,)),
            dma((ny - 1,)),
            dma((n_chunk,)),
            dma((n_chunk,)),
            dma((n_chunk * (nx - 1),)),
            dma((n_chunk * (nx - 1),)),
            dma((n_col,)),
            dma((n_col,)),
            dma((n_m,)),
            dma((n_m,)),
        ],
        compiler_params=pltpu.CompilerParams(
            collective_id=0, has_side_effects=True, vmem_limit_bytes=56 << 20
        ),
        name="round",
    )(
        frontal,
        sample_cols.T,
        leaf_first,
        jnp.pad(leaf_first.reshape(1, leaves), pad),
        jnp.pad(leaf_owner.reshape(1, leaves), pad),
        jnp.pad(skeleton.T, pad),
    )
    samples, interp, worst = pl.pallas_call(
        finish,
        out_shape=(
            jax.ShapeDtypeStruct((p_all, cap), F32),
            jax.ShapeDtypeStruct((skel, cap), F32),
            jax.ShapeDtypeStruct((1, 1), F32),
        ),
        in_specs=[vmem] * 3,
        out_specs=(vmem,) * 3,
        name="finish",
    )(*results)
    return samples, interp, worst.reshape(1)


def solution(mesh):
    return jax.shard_map(
        local,
        mesh=mesh,
        in_specs=(P("row", "col"), P(("col", "row"), None), P(), P(), P()),
        out_specs=(P("row", "col"), P("row", "col"), P()),
        check_vma=False,
    )
```

```python
import functools
import math

import jax
import jax.numpy as jnp
from jax import lax
from jax.experimental import pallas as pl
from jax.experimental.pallas import tpu as pltpu
from jax.sharding import PartitionSpec as P

UNIT = 32
RUN = 256
LANES = 128
LEAF_MOST = 4
F32 = jnp.float32
I32 = jnp.int32
MESH = pl.DeviceIdType.MESH
HI = lax.Precision.HIGHEST
NT = (((1,), (1,)), ((), ()))
NN = (((1,), (0,)), ((), ()))


def dot(a, b, dims, precision=None):
    return lax.dot_general(a, b, dims, precision=precision, preferred_element_type=F32)


def iota(shape, axis):
    return lax.broadcasted_iota(I32, shape, axis)


def out_kind(*shapes):
    return tuple(pltpu.VMEM(s, F32) for s in shapes)


def kernel(
    cfg,
    frontal,
    piece,
    lf_h1,
    lf_h,
    lo_h,
    sk_h,
    samples_out,
    interp_out,
    worst_out,
    a_v,
    pt,
    lf_s,
    lf_v,
    lo_v,
    sk_v,
    part,
    cx,
    s1,
    ph1,
    rot,
    pk,
    rx,
    table_v,
    table_s,
    w0,
    w1,
    w2,
    w3,
    a_sem,
    l_sem,
    t_sem,
    near_sem,
    pc_send,
    pc_recv,
    cx_send,
    cx_recv,
    p1_send,
    p1_recv,
    o_send,
    o_recv,
    m_send,
    m_recv,
):
    (rows, width, p_all, ny, nx, leaves_group, skel, cap, chunk) = cfg
    n_chunk = rows // chunk
    per_run = chunk // RUN
    tiles = rows // LANES
    half_p = p_all // 2
    sl = half_p // nx
    owners = 2 * nx
    n_col = owners * nx
    per_owner = cap // UNIT
    depth = width // ny

    g = lax.axis_index("row")
    me = lax.axis_index("col")
    core = lax.rem(me, 2)
    z = lax.rem(me // 2, nx)
    x = me // (2 * nx)
    q = jnp.where(core == 0, x, z)
    j_x = x * 2 + core

    def col_of(xx, zz, cc):
        return (xx * nx + zz) * 2 + cc

    def ring_a(pos):
        return col_of(jnp.where(core == 0, pos, x), jnp.where(core == 0, z, pos), core)

    def remote(src, dst, send_at, recv_at, row, col):
        return pltpu.make_async_remote_copy(
            src_ref=src,
            dst_ref=dst,
            send_sem=send_at,
            recv_sem=recv_at,
            device_id=(row, col),
            device_id_type=MESH,
        )

    def signal(sem, row, col):
        pl.semaphore_signal(sem, inc=1, device_id=(row, col), device_id_type=MESH)

    barrier = pltpu.get_barrier_semaphore()
    count = 0
    for d in range(1, ny):
        signal(barrier, lax.rem(g + d, ny), me)
        count += 1
    for d in range(1, owners):
        j = lax.rem(j_x + d, owners)
        signal(barrier, g, col_of(j // 2, z, lax.rem(j, 2)))
        count += 1
    for d in range(1, nx):
        for cc in range(2):
            signal(barrier, g, col_of(x, lax.rem(z + d, nx), cc))
            count += 1

    def load(i):
        at = pl.ds(pl.multiple_of(i * chunk, chunk), chunk)
        return pltpu.make_async_copy(frontal.at[at], a_v.at[at], a_sem.at[i])

    own_at = pl.ds(pl.multiple_of(g * depth, LANES), depth)
    small = [
        pltpu.make_async_copy(piece, pt.at[:, own_at], l_sem.at[0]),
        pltpu.make_async_copy(lf_h1, lf_s, l_sem.at[1]),
        pltpu.make_async_copy(lf_h, lf_v, l_sem.at[2]),
        pltpu.make_async_copy(lo_h, lo_v, l_sem.at[3]),
        pltpu.make_async_copy(sk_h, sk_v, l_sem.at[4]),
    ]
    for c in small:
        c.start()
    for i in range(n_chunk):
        load(i).start()
    pl.semaphore_wait(barrier, count)

    drains = []

    def send(copy):
        copy().start()
        drains.append(lambda: copy().wait_send())

    def piece_copy(d):
        to = lax.rem(g + d, ny)
        return remote(piece, pt.at[:, own_at], pc_send.at[d - 1], pc_recv.at[d - 1], to, me)

    turns = sorted(range(1, ny), key=lambda d: min(d, ny - d))
    for d in turns:
        send(functools.partial(piece_copy, d))

    for d in range(1, nx):
        signal(near_sem, g, col_of(x, lax.rem(z + d, nx), core))
    for d in range(1, ny):
        signal(near_sem, lax.rem(g + d, ny), me)

    for c in small:
        c.wait()
    nl = leaves_group
    lane = iota((1, LANES), 1)

    def group_lanes(v):
        out = None
        for gi in range(ny):
            part_v = v if gi == 0 else pltpu.roll(v, v.shape[1] - gi * nl, axis=1)
            part_v = part_v[:, :LANES]
            out = part_v if out is None else jnp.where(g == gi, part_v, out)
        return out

    first = group_lanes(lf_v[...])
    owner = group_lanes(lo_v[...])
    real = lane < nl
    owner = jnp.where(real, owner, -1)
    fu = jnp.where(real, (first - g * rows) // UNIT, 0)
    nxt = pltpu.roll(fu, LANES - 1, axis=1)
    nxt = jnp.where(lane == nl - 1, rows // UNIT, nxt)
    su = jnp.where(real, nxt - fu, 0)
    owner_t = jnp.transpose(jnp.broadcast_to(owner, (LANES, LANES)))
    fu_t = jnp.transpose(jnp.broadcast_to(fu, (LANES, LANES)))
    su_t = jnp.transpose(jnp.broadcast_to(su, (LANES, LANES)))
    li = iota((LANES, LANES), 0)
    lj = iota((LANES, LANES), 1)
    same = owner == owner_t
    before = same & (li < lj)
    after = same & (lj < li)
    off = jnp.sum(jnp.where(before, su_t, 0), axis=0, keepdims=True)
    rank = jnp.sum(jnp.where(before, 1, 0), axis=0, keepdims=True)
    off_t = jnp.sum(jnp.where(after, su, 0), axis=1, keepdims=True)
    rank_t = jnp.sum(jnp.where(after, 1, 0), axis=1, keepdims=True)
    dst = iota((1, n_col * per_owner), 1)
    d_owner = dst // per_owner
    d_su = lax.rem(dst, per_owner)
    o1 = owner_t[:, :1]
    f1 = fu_t[:, :1]
    u1 = su_t[:, :1]
    hit = (o1 == d_owner) & (off_t <= d_su) & (d_su < off_t + u1)
    src = jnp.sum(jnp.where(hit, f1 + d_su - off_t + 1, 0), axis=0, keepdims=True) - 1
    per_tile = LANES // UNIT
    turn = lax.rem(d_su - src + 8 * per_tile * rows, per_tile)
    entry = jnp.where(src >= 0, turn * tiles + src // per_tile, per_tile * tiles)
    table_v[...] = entry
    to_smem = pltpu.make_async_copy(table_v, table_s, t_sem)
    to_smem.start()

    slot = iota((1, cap), 1)
    slot_u = slot // UNIT
    mine_t = (o1 == me) & (off_t <= slot_u) & (slot_u < off_t + u1)
    slot_rank = jnp.sum(jnp.where(mine_t, rank_t + 1, 0), axis=0, keepdims=True) - 1
    sk = group_lanes(sk_v[...])
    sk_slot = sk - first + off * UNIT + 1
    cols = []
    for k in range(LEAF_MOST):
        pick_k = (owner == me) & (rank == k)
        cols.append(jnp.sum(jnp.where(pick_k, sk_slot, 0), axis=1, keepdims=True))
    sk_col = jnp.concatenate(cols, axis=0)
    hot = jnp.where(sk_col == slot + 1, 1.0, 0.0).astype(F32)
    ki = LEAF_MOST * skel
    row_k = iota((ki, 1), 0) // skel

    def mask_run(t):
        run = g * (rows // RUN) + t
        blocks = width // RUN

        @pl.when(run // blocks == me)
        def _():
            r0 = pl.multiple_of(t * RUN, RUN)
            c0 = pl.multiple_of(lax.rem(run, blocks) * RUN, RUN)
            ri = iota((RUN, RUN), 0) + run * RUN
            ci = iota((RUN, RUN), 1) + run * RUN
            rl = jnp.zeros((RUN, RUN), I32)
            cl = jnp.zeros((RUN, RUN), I32)
            for k in range(1, 4):
                edge = lf_s[run * 4 + k]
                rl = rl + jnp.where(ri >= edge, 1, 0)
                cl = cl + jnp.where(ci >= edge, 1, 0)
            block = a_v[pl.ds(r0, RUN), pl.ds(c0, RUN)].astype(F32)
            a_v[pl.ds(r0, RUN), pl.ds(c0, RUN)] = jnp.where(rl == cl, 0.0, block).astype(jnp.bfloat16)

    def product(at, d):
        k_at = pl.ds(pl.multiple_of(lax.rem(g + d, ny) * depth, LANES), depth)
        return dot(pt[:, k_at], a_v[at, k_at], NT)

    for i in range(n_chunk):
        load(i).wait()
        for t in range(per_run):
            mask_run(i * per_run + t)
        at = pl.ds(i * chunk, chunk)
        part[:, at] = product(at, 0)

    sibling = col_of(x, z, 1 - core)

    def core_copy(i):
        at = pl.ds(pl.multiple_of(i * chunk, chunk), chunk)
        theirs = pl.ds(pl.multiple_of((1 - core) * half_p, half_p), half_p)
        return remote(part.at[theirs, at], cx.at[:, at], cx_send.at[i], cx_recv.at[i], g, sibling)

    for d in turns[:-1]:
        piece_copy(d).wait_recv()
        part[...] += product(pl.ds(0, rows), ny - d)
    piece_copy(turns[-1]).wait_recv()
    for i in range(n_chunk):
        at = pl.ds(i * chunk, chunk)
        part[:, at] += product(at, ny - turns[-1])
        core_copy(i).start()

    def first_copy(i, d):
        to = lax.rem(q + d, nx)
        at = pl.ds(pl.multiple_of(i * chunk, chunk), chunk)
        rows_at = pl.ds(pl.multiple_of(to * sl, sl), sl)
        s = i * (nx - 1) + d - 1
        return remote(s1.at[rows_at, at], ph1.at[d - 1, :, at], p1_send.at[s], p1_recv.at[s], g, ring_a(to))

    def core_sum(i, carry):
        at = pl.ds(pl.multiple_of(i * chunk, chunk), chunk)
        own = pl.ds(pl.multiple_of(core * half_p, half_p), half_p)
        core_copy(i).wait_recv()
        s1[:, at] = part[own, at] + cx[:, at]
        for d in range(1, nx):
            first_copy(i, d).start()
        return carry

    def drain(i, carry):
        core_copy(i).wait_send()
        for d in range(1, nx):
            first_copy(i, d).wait_send()
        return carry

    lax.fori_loop(0, n_chunk, core_sum, 0)
    drains.append(lambda: lax.fori_loop(0, n_chunk, drain, 0))

    rot[per_tile * tiles] = jnp.zeros((sl, LANES), F32)

    def first_sum(i, carry):
        for d in range(1, nx):
            first_copy(i, d).wait_recv()
        own = pl.ds(pl.multiple_of(q * sl, sl), sl)
        for t in range(chunk // LANES):
            at = pl.ds(pl.multiple_of(i * chunk + t * LANES, LANES), LANES)
            v = s1[own, at]
            for d in range(1, nx):
                v = v + ph1[d - 1, :, at]
            tile = i * (chunk // LANES) + t
            rot[tile] = v
            for k in range(1, per_tile):
                rot[k * tiles + tile] = pltpu.roll(v, k * UNIT, axis=1)
        return carry

    lax.fori_loop(0, n_chunk, first_sum, 0)

    to_smem.wait()
    pl.semaphore_wait(near_sem, nx - 1 + ny - 1)
    lane_u = iota((sl, LANES), 1) // UNIT

    def there(k):
        dx, dz, dc = k
        return col_of(lax.rem(x + dx, nx), lax.rem(z + dz, nx), lax.rem(core + dc, 2))

    def owner_copy(n, k):
        return remote(pk.at[n], rx.at[me], o_send.at[n], o_recv.at[me], g, there(k))

    def owner_wait(n, k):
        frm = there(k)
        return remote(pk.at[n], rx.at[frm], o_send.at[n], o_recv.at[frm], g, frm)

    def block_of(o, h):
        base = o * per_owner + h * per_tile
        v = rot[table_s[0, base]]
        for k in range(1, per_tile):
            v = jnp.where(lane_u == k, rot[table_s[0, base + k]], v)
        return v

    steps = [(dx, dz, dc) for dx in range(nx) for dz in range(nx) for dc in range(2)]
    steps.sort(key=lambda k: -(min(k[0], nx - k[0]) + min(k[1], nx - k[1])))
    steps = [k for k in steps if k != (0, 0, 0)]
    for n, k in enumerate(steps):
        o = there(k)
        for h in range(cap // LANES):
            pk[n, :, h * LANES : (h + 1) * LANES] = block_of(o, h)
        send(functools.partial(owner_copy, n, k))
    for h in range(cap // LANES):
        rx[me, :, h * LANES : (h + 1) * LANES] = block_of(me, h)
    for n, k in reversed(list(enumerate(steps))):
        owner_wait(n, k).wait_recv()

    def total(ids):
        v = rx[ids[0]]
        for s in ids[1:]:
            v = v + rx[s]
        return v

    m = jnp.concatenate(
        [total([col_of(a, b, 0) for b in range(nx)]) for a in range(nx)]
        + [total([col_of(b, a, 1) for b in range(nx)]) for a in range(nx)],
        axis=0,
    )

    samples_out[...] = m
    pick = dot(hot, m, NT, HI)
    pick_t = dot(m, hot, NT, HI)
    rhs = dot(pick, m, NN, HI)
    gram = dot(pick, pick, NT, HI)
    col_k = iota((1, ki), 1) // skel
    in_block = row_k == col_k
    gram = jnp.where(in_block, gram, 0.0)
    folded = gram[:skel]
    for k in range(1, LEAF_MOST):
        folded = folded + gram[k * skel : (k + 1) * skel]
    here = jnp.concatenate(
        [jnp.broadcast_to(jnp.where(c[:1] > 0, 1, 0), (1, skel)) for c in cols], axis=1
    )
    eye_i = iota((skel, ki), 0)
    eye_r = lax.rem(iota((skel, ki), 1), skel)
    a = []
    for j in range(skel):
        v = None
        for k in range(LEAF_MOST):
            c = jnp.broadcast_to(folded[:, k * skel + j : k * skel + j + 1], (skel, ki))
            v = c if v is None else jnp.where(col_k == k, c, v)
        a.append(v + jnp.where((eye_i == j) & (here == 0), 1.0, 0.0))
    inv = jnp.where(eye_i == eye_r, 1.0, 0.0).astype(F32)
    for s in range(skel):
        col = a[s]
        rcp = 1.0 / col[s : s + 1]
        at_s = eye_i == s
        for j in range(s + 1, skel):
            t = a[j][s : s + 1] * rcp
            a[j] = jnp.where(at_s, t, a[j] - col * t)
        t = inv[s : s + 1] * rcp
        inv = jnp.where(at_s, t, inv - col * t)
    inv_all = jnp.where(in_block, jnp.concatenate([inv] * LEAF_MOST, axis=0), 0.0)
    rhs = jnp.where(row_k == slot_rank, rhs, 0.0)
    coeff = dot(inv_all, rhs, NN, HI)
    resid = m - dot(pick_t, coeff, NN, HI)
    err = jnp.sum(resid * resid, axis=0, keepdims=True)
    norm = jnp.sum(m * m, axis=0, keepdims=True)
    of_k = iota((8, 1), 0) == slot_rank
    err = jnp.sum(jnp.where(of_k, err, 0.0), axis=1, keepdims=True)
    norm = jnp.sum(jnp.where(of_k, norm, 0.0), axis=1, keepdims=True)
    ratio = jnp.sqrt(err) / jnp.sqrt(norm + 1e-06)
    w0[...] = jnp.broadcast_to(jnp.max(ratio, axis=0, keepdims=True), w0.shape)

    def m1(d):
        j = lax.rem(j_x + d, owners)
        to = col_of(j // 2, z, lax.rem(j, 2))
        return remote(w0.at[:1], w1.at[d - 1, :1], m_send.at[d - 1], m_recv.at[d - 1], g, to)

    def m2(d):
        s = owners - 2 + d
        to_y = lax.rem(g + d // nx, ny)
        to = col_of(x, lax.rem(z + d % nx, nx), core)
        return remote(w2.at[:1], w3.at[d - 1, :1], m_send.at[s], m_recv.at[s], to_y, to)

    for d in range(1, owners):
        send(functools.partial(m1, d))
    folded_c = coeff[:skel]
    for k in range(1, LEAF_MOST):
        folded_c = folded_c + coeff[k * skel : (k + 1) * skel]
    interp_out[...] = folded_c
    for d in range(1, owners):
        m1(d).wait_recv()
    v = w0[:1]
    for d in range(1, owners):
        v = jnp.maximum(v, w1[d - 1, :1])
    w2[...] = jnp.broadcast_to(v, w2.shape)
    for d in range(1, nx * ny):
        send(functools.partial(m2, d))
    for f in drains:
        f()
    for d in range(1, nx * ny):
        m2(d).wait_recv()
    for d in range(1, nx * ny):
        v = jnp.maximum(v, w3[d - 1, :1])
    worst_out[...] = v


def finish(a_ref, b_ref, c_ref, a_out, b_out, c_out):
    a_out[...] = a_ref[...]
    b_out[...] = b_ref[...]
    c_out[...] = c_ref[:, :1]


def local(frontal, sample_cols, leaf_first, leaf_owner, skeleton):
    rows, width = frontal.shape
    p_all = sample_cols.shape[1]
    leaves, skel = skeleton.shape
    n_col = lax.axis_size("col")
    ny = lax.axis_size("row")
    nx = math.isqrt(n_col // 2)
    cap = 2 * rows // n_col
    chunk = 512
    n_chunk = rows // chunk
    tiles = rows // LANES
    half_p = p_all // 2
    sl = half_p // nx
    owners = 2 * nx
    cfg = (rows, width, p_all, ny, nx, leaves // ny, skel, cap, chunk)
    slots_all = n_col * cap // UNIT
    hbm = pl.BlockSpec(memory_space=pl.ANY)
    vmem = pl.BlockSpec(memory_space=pltpu.VMEM)
    dma = pltpu.SemaphoreType.DMA
    n_m = owners - 1 + nx * ny - 1
    pad = ((0, 0), (0, max(0, LANES - leaves)))
    wide = leaves + pad[1][1]
    results = pl.pallas_call(
        functools.partial(kernel, cfg),
        out_shape=out_kind((p_all, cap), (skel, cap), (1, LANES)),
        in_specs=[hbm] * 6,
        out_specs=(vmem, vmem, vmem),
        scratch_shapes=[
            pltpu.VMEM((rows, width), jnp.bfloat16),
            pltpu.VMEM((p_all, width), jnp.bfloat16),
            pltpu.SMEM((leaves,), I32),
            pltpu.VMEM((1, wide), I32),
            pltpu.VMEM((1, wide), I32),
            pltpu.VMEM((skel, wide), I32),
            pltpu.VMEM((p_all, rows), F32),
            pltpu.VMEM((half_p, rows), F32),
            pltpu.VMEM((half_p, rows), F32),
            pltpu.VMEM((nx - 1, sl, rows), F32),
            pltpu.VMEM((4 * tiles + 1, sl, LANES), F32),
            pltpu.VMEM((n_col - 1, sl, cap), F32),
            pltpu.VMEM((n_col, sl, cap), F32),
            pltpu.VMEM((1, slots_all), I32),
            pltpu.SMEM((1, slots_all), I32),
            pltpu.VMEM((8, LANES), F32),
            pltpu.VMEM((owners - 1, 8, LANES), F32),
            pltpu.VMEM((8, LANES), F32),
            pltpu.VMEM((nx * ny - 1, 8, LANES), F32),
            dma((n_chunk,)),
            dma((5,)),
            dma(()),
            pltpu.SemaphoreType.REGULAR,
            dma((ny - 1,)),
            dma((ny - 1,)),
            dma((n_chunk,)),
            dma((n_chunk,)),
            dma((n_chunk * (nx - 1),)),
            dma((n_chunk * (nx - 1),)),
            dma((n_col,)),
            dma((n_col,)),
            dma((n_m,)),
            dma((n_m,)),
        ],
        compiler_params=pltpu.CompilerParams(
            collective_id=0, has_side_effects=True, vmem_limit_bytes=56 << 20
        ),
        name="round",
    )(
        frontal,
        sample_cols.T,
        leaf_first,
        jnp.pad(leaf_first.reshape(1, leaves), pad),
        jnp.pad(leaf_owner.reshape(1, leaves), pad),
        jnp.pad(skeleton.T, pad),
    )
    samples, interp, worst = pl.pallas_call(
        finish,
        out_shape=(
            jax.ShapeDtypeStruct((p_all, cap), F32),
            jax.ShapeDtypeStruct((skel, cap), F32),
            jax.ShapeDtypeStruct((1, 1), F32),
        ),
        in_specs=[vmem] * 3,
        out_specs=(vmem,) * 3,
        name="finish",
    )(*(pltpu.with_memory_space_constraint(r, pltpu.VMEM) for r in results))
    return samples, interp, worst.reshape(1)


def solution(mesh):
    return jax.shard_map(
        local,
        mesh=mesh,
        in_specs=(P("row", "col"), P(("col", "row"), None), P(), P(), P()),
        out_specs=(P("row", "col"), P("row", "col"), P()),
        check_vma=False,
    )
```

```python
import functools
import math

import jax
import jax.numpy as jnp
from jax import lax
from jax.experimental import pallas as pl
from jax.experimental.pallas import tpu as pltpu
from jax.sharding import PartitionSpec as P

UNIT = 32
RUN = 256
LANES = 128
LEAF_MOST = 4
F32 = jnp.float32
I32 = jnp.int32
MESH = pl.DeviceIdType.MESH
HI = lax.Precision.HIGHEST
NT = (((1,), (1,)), ((), ()))
NN = (((1,), (0,)), ((), ()))


def dot(a, b, dims, precision=None):
    return lax.dot_general(a, b, dims, precision=precision, preferred_element_type=F32)


def iota(shape, axis):
    return lax.broadcasted_iota(I32, shape, axis)


def out_kind(*shapes):
    return tuple(pltpu.VMEM(s, F32) for s in shapes)


def kernel(
    cfg,
    frontal,
    piece,
    lf_h1,
    lf_h,
    lo_h,
    sk_h,
    samples_out,
    interp_out,
    worst_out,
    a_v,
    pt,
    lf_s,
    lf_v,
    lo_v,
    sk_v,
    part,
    cx,
    s1,
    ph1,
    rot,
    pk,
    rx,
    table_v,
    table_s,
    w0,
    w1,
    w2,
    w3,
    a_sem,
    l_sem,
    t_sem,
    near_sem,
    pc_send,
    pc_recv,
    cx_send,
    cx_recv,
    p1_send,
    p1_recv,
    o_send,
    o_recv,
    m_send,
    m_recv,
):
    (rows, width, p_all, ny, nx, leaves_group, skel, cap, chunk) = cfg
    n_chunk = rows // chunk
    per_run = chunk // RUN
    half = n_chunk // 2
    tiles = rows // LANES
    half_p = p_all // 2
    sl = half_p // nx
    owners = 2 * nx
    n_col = owners * nx
    per_owner = cap // UNIT
    depth = width // ny

    g = lax.axis_index("row")
    me = lax.axis_index("col")
    core = lax.rem(me, 2)
    z = lax.rem(me // 2, nx)
    x = me // (2 * nx)
    q = jnp.where(core == 0, x, z)
    j_x = x * 2 + core
    me_next = x * 2 * nx + z * 2 + 1 - core

    def col_of(xx, zz, cc):
        return (xx * nx + zz) * 2 + cc

    def ring_a(pos):
        return col_of(jnp.where(core == 0, pos, x), jnp.where(core == 0, z, pos), core)

    def remote(src, dst, send_at, recv_at, row, col):
        return pltpu.make_async_remote_copy(
            src_ref=src,
            dst_ref=dst,
            send_sem=send_at,
            recv_sem=recv_at,
            device_id=(row, col),
            device_id_type=MESH,
        )

    def signal(sem, row, col):
        pl.semaphore_signal(sem, inc=1, device_id=(row, col), device_id_type=MESH)

    barrier = pltpu.get_barrier_semaphore()
    count = 0
    for d in range(1, ny):
        signal(barrier, lax.rem(g + d, ny), me)
        count += 1
    for d in range(1, owners):
        j = lax.rem(j_x + d, owners)
        signal(barrier, g, col_of(j // 2, z, lax.rem(j, 2)))
        count += 1
    for d in range(1, nx):
        for cc in range(2):
            signal(barrier, g, col_of(x, lax.rem(z + d, nx), cc))
            count += 1

    def load(i):
        at = pl.ds(pl.multiple_of(i * chunk, chunk), chunk)
        return pltpu.make_async_copy(frontal.at[at], a_v.at[at], a_sem.at[i])

    own_at = pl.ds(pl.multiple_of(g * depth, LANES), depth)
    small = [
        pltpu.make_async_copy(piece, pt.at[:, own_at], l_sem.at[0]),
        pltpu.make_async_copy(lf_h1, lf_s, l_sem.at[1]),
        pltpu.make_async_copy(lf_h, lf_v, l_sem.at[2]),
        pltpu.make_async_copy(lo_h, lo_v, l_sem.at[3]),
        pltpu.make_async_copy(sk_h, sk_v, l_sem.at[4]),
    ]
    for c in small:
        c.start()
    for i in range(n_chunk):
        load(i).start()
    pl.semaphore_wait(barrier, count)

    drains = []

    def piece_copy(d):
        to = lax.rem(g + d, ny)
        return remote(piece, pt.at[:, own_at], pc_send, pc_recv.at[d - 1], to, me)

    def piece_sends():
        at = pl.ds(0, (ny - 1) * depth)
        remote(pt.at[:, at], pt.at[:, at], pc_send, pc_recv.at[0], g, me_next).wait_send()

    turns = sorted(range(1, ny), key=lambda d: min(d, ny - d))
    for d in turns:
        piece_copy(d).start()
    drains.append(piece_sends)

    for d in range(1, nx):
        signal(near_sem, g, col_of(x, lax.rem(z + d, nx), core))
    for d in range(1, ny):
        signal(near_sem, lax.rem(g + d, ny), me)

    for c in small[:2]:
        c.wait()

    def mask_run(t):
        run = g * (rows // RUN) + t
        blocks = width // RUN

        @pl.when(run // blocks == me)
        def _():
            r0 = pl.multiple_of(t * RUN, RUN)
            c0 = pl.multiple_of(lax.rem(run, blocks) * RUN, RUN)
            ri = iota((RUN, RUN), 0) + run * RUN
            ci = iota((RUN, RUN), 1) + run * RUN
            rl = jnp.zeros((RUN, RUN), I32)
            cl = jnp.zeros((RUN, RUN), I32)
            for k in range(1, 4):
                edge = lf_s[run * 4 + k]
                rl = rl + jnp.where(ri >= edge, 1, 0)
                cl = cl + jnp.where(ci >= edge, 1, 0)
            block = a_v[pl.ds(r0, RUN), pl.ds(c0, RUN)].astype(F32)
            a_v[pl.ds(r0, RUN), pl.ds(c0, RUN)] = jnp.where(rl == cl, 0.0, block).astype(jnp.bfloat16)

    def product(at, d):
        k_at = pl.ds(pl.multiple_of(lax.rem(g + d, ny) * depth, LANES), depth)
        return dot(pt[:, k_at], a_v[at, k_at], NT)

    for h in range(2):
        for i in range(h * half, (h + 1) * half):
            load(i).wait()
        for t in range(h * half * per_run, (h + 1) * half * per_run):
            mask_run(t)
        at = pl.ds(h * half * chunk, half * chunk)
        part[:, at] = product(at, 0)

    sibling = col_of(x, z, 1 - core)

    def core_copy(i):
        at = pl.ds(pl.multiple_of(i * chunk, chunk), chunk)
        theirs = pl.ds(pl.multiple_of((1 - core) * half_p, half_p), half_p)
        return remote(part.at[theirs, at], cx.at[:, at], cx_send, cx_recv.at[i], g, sibling)

    for d in turns[:-1]:
        piece_copy(d).wait_recv()
        part[...] += product(pl.ds(0, rows), ny - d)
    piece_copy(turns[-1]).wait_recv()
    for h in range(2):
        at = pl.ds(h * half * chunk, half * chunk)
        part[:, at] += product(at, ny - turns[-1])
        for i in range(h * half, (h + 1) * half):
            core_copy(i).start()
    drains.append(lambda: remote(cx, cx, cx_send, cx_recv.at[0], g, sibling).wait_send())

    def first_copy(i, d):
        to = lax.rem(q + d, nx)
        at = pl.ds(pl.multiple_of(i * chunk, chunk), chunk)
        rows_at = pl.ds(pl.multiple_of(to * sl, sl), sl)
        return remote(s1.at[rows_at, at], ph1.at[d - 1, :, at], p1_send, p1_recv.at[i], g, ring_a(to))

    def core_sum(i, carry):
        at = pl.ds(pl.multiple_of(i * chunk, chunk), chunk)
        own = pl.ds(pl.multiple_of(core * half_p, half_p), half_p)
        core_copy(i).wait_recv()
        s1[:, at] = part[own, at] + cx[:, at]
        for d in sorted(range(1, nx), key=lambda d: -min(d, nx - d)):
            first_copy(i, d).start()
        return carry

    lax.fori_loop(0, n_chunk, core_sum, 0)
    drains.append(lambda: remote(ph1, ph1, p1_send, p1_recv.at[0], g, sibling).wait_send())

    for c in small[2:]:
        c.wait()
    nl = leaves_group
    lane = iota((1, LANES), 1)

    def group_lanes(v):
        out = None
        for gi in range(ny):
            part_v = v if gi == 0 else pltpu.roll(v, v.shape[1] - gi * nl, axis=1)
            part_v = part_v[:, :LANES]
            out = part_v if out is None else jnp.where(g == gi, part_v, out)
        return out

    first = group_lanes(lf_v[...])
    owner = group_lanes(lo_v[...])
    real = lane < nl
    owner = jnp.where(real, owner, -1)
    fu = jnp.where(real, (first - g * rows) // UNIT, 0)
    nxt = pltpu.roll(fu, LANES - 1, axis=1)
    nxt = jnp.where(lane == nl - 1, rows // UNIT, nxt)
    su = jnp.where(real, nxt - fu, 0)
    owner_t = jnp.transpose(jnp.broadcast_to(owner, (LANES, LANES)))
    fu_t = jnp.transpose(jnp.broadcast_to(fu, (LANES, LANES)))
    su_t = jnp.transpose(jnp.broadcast_to(su, (LANES, LANES)))
    li = iota((LANES, LANES), 0)
    lj = iota((LANES, LANES), 1)
    same = owner == owner_t
    before = same & (li < lj)
    after = same & (lj < li)
    off = jnp.sum(jnp.where(before, su_t, 0), axis=0, keepdims=True)
    rank = jnp.sum(jnp.where(before, 1, 0), axis=0, keepdims=True)
    off_t = jnp.sum(jnp.where(after, su, 0), axis=1, keepdims=True)
    rank_t = jnp.sum(jnp.where(after, 1, 0), axis=1, keepdims=True)
    dst = iota((1, n_col * per_owner), 1)
    d_owner = dst // per_owner
    d_su = lax.rem(dst, per_owner)
    o1 = owner_t[:, :1]
    f1 = fu_t[:, :1]
    u1 = su_t[:, :1]
    hit = (o1 == d_owner) & (off_t <= d_su) & (d_su < off_t + u1)
    src = jnp.sum(jnp.where(hit, f1 + d_su - off_t + 1, 0), axis=0, keepdims=True) - 1
    per_tile = LANES // UNIT
    turn = lax.rem(d_su - src + 8 * per_tile * rows, per_tile)
    entry = jnp.where(src >= 0, turn * tiles + src // per_tile, per_tile * tiles)
    table_v[...] = entry
    to_smem = pltpu.make_async_copy(table_v, table_s, t_sem)
    to_smem.start()

    slot = iota((1, cap), 1)
    slot_u = slot // UNIT
    mine_t = (o1 == me) & (off_t <= slot_u) & (slot_u < off_t + u1)
    slot_rank = jnp.sum(jnp.where(mine_t, rank_t + 1, 0), axis=0, keepdims=True) - 1
    sk = group_lanes(sk_v[...])
    sk_slot = sk - first + off * UNIT + 1
    cols = []
    for k in range(LEAF_MOST):
        pick_k = (owner == me) & (rank == k)
        cols.append(jnp.sum(jnp.where(pick_k, sk_slot, 0), axis=1, keepdims=True))
    sk_col = jnp.concatenate(cols, axis=0)
    hot = jnp.where(sk_col == slot + 1, 1.0, 0.0).astype(F32)
    ki = LEAF_MOST * skel
    row_k = iota((ki, 1), 0) // skel

    rot[per_tile * tiles] = jnp.zeros((sl, LANES), F32)

    def first_sum(i, carry):
        every = ph1.at[:, :, pl.ds(pl.multiple_of(i * chunk, chunk), chunk)]
        remote(every, every, p1_send, p1_recv.at[i], g, sibling).wait_recv()
        own = pl.ds(pl.multiple_of(q * sl, sl), sl)
        for t in range(chunk // LANES):
            at = pl.ds(pl.multiple_of(i * chunk + t * LANES, LANES), LANES)
            v = s1[own, at]
            for d in range(1, nx):
                v = v + ph1[d - 1, :, at]
            tile = i * (chunk // LANES) + t
            rot[tile] = v
            for k in range(1, per_tile):
                rot[k * tiles + tile] = pltpu.roll(v, k * UNIT, axis=1)
        return carry

    lax.fori_loop(0, n_chunk, first_sum, 0)

    to_smem.wait()
    pl.semaphore_wait(near_sem, nx - 1 + ny - 1)
    lane_u = iota((sl, LANES), 1) // UNIT

    def there(k):
        dx, dz, dc = k
        return col_of(lax.rem(x + dx, nx), lax.rem(z + dz, nx), lax.rem(core + dc, 2))

    def owner_copy(n, k):
        return remote(pk.at[n], rx.at[me], o_send, o_recv, g, there(k))

    def block_of(o, h):
        base = o * per_owner + h * per_tile
        v = rot[table_s[0, base]]
        for k in range(1, per_tile):
            v = jnp.where(lane_u == k, rot[table_s[0, base + k]], v)
        return v

    steps = [(dx, dz, dc) for dx in range(nx) for dz in range(nx) for dc in range(2)]
    steps.sort(key=lambda k: -(min(k[0], nx - k[0]) + min(k[1], nx - k[1])))
    steps = [k for k in steps if k != (0, 0, 0)]
    for n, k in enumerate(steps):
        o = there(k)
        for h in range(cap // LANES):
            pk[n, :, h * LANES : (h + 1) * LANES] = block_of(o, h)
        owner_copy(n, k).start()
    for h in range(cap // LANES):
        rx[me, :, h * LANES : (h + 1) * LANES] = block_of(me, h)
    blocks_in = remote(pk, rx.at[: n_col - 1], o_send, o_recv, g, sibling)
    blocks_in.wait_recv()
    drains.append(blocks_in.wait_send)

    def total(ids):
        v = rx[ids[0]]
        for s in ids[1:]:
            v = v + rx[s]
        return v

    m = jnp.concatenate(
        [total([col_of(a, b, 0) for b in range(nx)]) for a in range(nx)]
        + [total([col_of(b, a, 1) for b in range(nx)]) for a in range(nx)],
        axis=0,
    )

    samples_out[...] = m
    pick = dot(hot, m, NT, HI)
    pick_t = dot(m, hot, NT, HI)
    rhs = dot(pick, m, NN, HI)
    gram = dot(pick, pick, NT, HI)
    col_k = iota((1, ki), 1) // skel
    in_block = row_k == col_k
    gram = jnp.where(in_block, gram, 0.0)
    folded = gram[:skel]
    for k in range(1, LEAF_MOST):
        folded = folded + gram[k * skel : (k + 1) * skel]
    here = jnp.concatenate(
        [jnp.broadcast_to(jnp.where(c[:1] > 0, 1, 0), (1, skel)) for c in cols], axis=1
    )
    eye_i = iota((skel, ki), 0)
    eye_r = lax.rem(iota((skel, ki), 1), skel)
    a = []
    for j in range(skel):
        v = None
        for k in range(LEAF_MOST):
            c = jnp.broadcast_to(folded[:, k * skel + j : k * skel + j + 1], (skel, ki))
            v = c if v is None else jnp.where(col_k == k, c, v)
        a.append(v + jnp.where((eye_i == j) & (here == 0), 1.0, 0.0))
    inv = jnp.where(eye_i == eye_r, 1.0, 0.0).astype(F32)
    for s in range(skel):
        col = a[s]
        rcp = 1.0 / col[s : s + 1]
        at_s = eye_i == s
        for j in range(s + 1, skel):
            t = a[j][s : s + 1] * rcp
            a[j] = jnp.where(at_s, t, a[j] - col * t)
        t = inv[s : s + 1] * rcp
        inv = jnp.where(at_s, t, inv - col * t)
    inv_all = jnp.where(in_block, jnp.concatenate([inv] * LEAF_MOST, axis=0), 0.0)
    rhs = jnp.where(row_k == slot_rank, rhs, 0.0)
    coeff = dot(inv_all, rhs, NN, HI)
    resid = m - dot(pick_t, coeff, NN, HI)
    err = jnp.sum(resid * resid, axis=0, keepdims=True)
    norm = jnp.sum(m * m, axis=0, keepdims=True)
    of_k = iota((8, 1), 0) == slot_rank
    err = jnp.sum(jnp.where(of_k, err, 0.0), axis=1, keepdims=True)
    norm = jnp.sum(jnp.where(of_k, norm, 0.0), axis=1, keepdims=True)
    ratio = jnp.sqrt(err) / jnp.sqrt(norm + 1e-06)
    w0[...] = jnp.broadcast_to(jnp.max(ratio, axis=0, keepdims=True), w0.shape)

    def m1(d):
        j = lax.rem(j_x + d, owners)
        to = col_of(j // 2, z, lax.rem(j, 2))
        return remote(w0.at[:1], w1.at[d - 1, :1], m_send.at[0], m_recv.at[0], g, to)

    def m2(d):
        to_y = lax.rem(g + d // nx, ny)
        to = col_of(x, lax.rem(z + d % nx, nx), core)
        return remote(w2.at[:1], w3.at[d - 1, :1], m_send.at[1], m_recv.at[1], to_y, to)

    for d in sorted(range(1, owners), key=lambda d: -min(d, owners - d)):
        m1(d).start()
    folded_c = coeff[:skel]
    for k in range(1, LEAF_MOST):
        folded_c = folded_c + coeff[k * skel : (k + 1) * skel]
    interp_out[...] = folded_c
    all1 = remote(w1.at[:, :1], w1.at[:, :1], m_send.at[0], m_recv.at[0], g, sibling)
    all1.wait_recv()
    v = w0[:1]
    for d in range(1, owners):
        v = jnp.maximum(v, w1[d - 1, :1])
    w2[...] = jnp.broadcast_to(v, w2.shape)
    for d in sorted(range(1, nx * ny), key=lambda d: -min(d % nx, nx - d % nx) - min(d // nx, ny - d // nx)):
        m2(d).start()
    for f in drains:
        f()
    all1.wait_send()
    all2 = remote(w3.at[:, :1], w3.at[:, :1], m_send.at[1], m_recv.at[1], g, sibling)
    all2.wait_send()
    all2.wait_recv()
    for d in range(1, nx * ny):
        v = jnp.maximum(v, w3[d - 1, :1])
    worst_out[...] = v


def finish(a_ref, b_ref, c_ref, a_out, b_out, c_out):
    a_out[...] = a_ref[...]
    b_out[...] = b_ref[...]
    c_out[...] = c_ref[:, :1]


def local(frontal, sample_cols, leaf_first, leaf_owner, skeleton):
    rows, width = frontal.shape
    p_all = sample_cols.shape[1]
    leaves, skel = skeleton.shape
    n_col = lax.axis_size("col")
    ny = lax.axis_size("row")
    nx = math.isqrt(n_col // 2)
    cap = 2 * rows // n_col
    chunk = 512
    n_chunk = rows // chunk
    tiles = rows // LANES
    half_p = p_all // 2
    sl = half_p // nx
    owners = 2 * nx
    cfg = (rows, width, p_all, ny, nx, leaves // ny, skel, cap, chunk)
    slots_all = n_col * cap // UNIT
    hbm = pl.BlockSpec(memory_space=pl.ANY)
    vmem = pl.BlockSpec(memory_space=pltpu.VMEM)
    dma = pltpu.SemaphoreType.DMA
    pad = ((0, 0), (0, max(0, LANES - leaves)))
    wide = leaves + pad[1][1]
    results = pl.pallas_call(
        functools.partial(kernel, cfg),
        out_shape=out_kind((p_all, cap), (skel, cap), (1, LANES)),
        in_specs=[hbm] * 6,
        out_specs=(vmem, vmem, vmem),
        scratch_shapes=[
            pltpu.VMEM((rows, width), jnp.bfloat16),
            pltpu.VMEM((p_all, width), jnp.bfloat16),
            pltpu.SMEM((leaves,), I32),
            pltpu.VMEM((1, wide), I32),
            pltpu.VMEM((1, wide), I32),
            pltpu.VMEM((skel, wide), I32),
            pltpu.VMEM((p_all, rows), F32),
            pltpu.VMEM((half_p, rows), F32),
            pltpu.VMEM((half_p, rows), F32),
            pltpu.VMEM((nx - 1, sl, rows), F32),
            pltpu.VMEM((4 * tiles + 1, sl, LANES), F32),
            pltpu.VMEM((n_col - 1, sl, cap), F32),
            pltpu.VMEM((n_col, sl, cap), F32),
            pltpu.VMEM((1, slots_all), I32),
            pltpu.SMEM((1, slots_all), I32),
            pltpu.VMEM((8, LANES), F32),
            pltpu.VMEM((owners - 1, 8, LANES), F32),
            pltpu.VMEM((8, LANES), F32),
            pltpu.VMEM((nx * ny - 1, 8, LANES), F32),
            dma((n_chunk,)),
            dma((5,)),
            dma(()),
            pltpu.SemaphoreType.REGULAR,
            dma(()),
            dma((ny - 1,)),
            dma(()),
            dma((n_chunk,)),
            dma(()),
            dma((n_chunk,)),
            dma(()),
            dma(()),
            dma((2,)),
            dma((2,)),
        ],
        compiler_params=pltpu.CompilerParams(
            collective_id=0, has_side_effects=True, vmem_limit_bytes=56 << 20
        ),
        name="round",
    )(
        frontal,
        sample_cols.T,
        leaf_first,
        jnp.pad(leaf_first.reshape(1, leaves), pad),
        jnp.pad(leaf_owner.reshape(1, leaves), pad),
        jnp.pad(skeleton.T, pad),
    )
    samples, interp, worst = pl.pallas_call(
        finish,
        out_shape=(
            jax.ShapeDtypeStruct((p_all, cap), F32),
            jax.ShapeDtypeStruct((skel, cap), F32),
            jax.ShapeDtypeStruct((1, 1), F32),
        ),
        in_specs=[vmem] * 3,
        out_specs=(vmem,) * 3,
        name="finish",
    )(*(pltpu.with_memory_space_constraint(r, pltpu.VMEM) for r in results))
    return samples, interp, worst.reshape(1)


def solution(mesh):
    return jax.shard_map(
        local,
        mesh=mesh,
        in_specs=(P("row", "col"), P(("col", "row"), None), P(), P(), P()),
        out_specs=(P("row", "col"), P("row", "col"), P()),
        check_vma=False,
    )
```

```python
import functools
import math

import jax
import jax.numpy as jnp
from jax import lax
from jax.experimental import pallas as pl
from jax.experimental.pallas import tpu as pltpu
from jax.sharding import PartitionSpec as P

UNIT = 32
RUN = 256
LANES = 128
LEAF_MOST = 4
F32 = jnp.float32
I32 = jnp.int32
MESH = pl.DeviceIdType.MESH
HI = lax.Precision.HIGHEST
NT = (((1,), (1,)), ((), ()))
NN = (((1,), (0,)), ((), ()))


def dot(a, b, dims, precision=None):
    return lax.dot_general(a, b, dims, precision=precision, preferred_element_type=F32)


def iota(shape, axis):
    return lax.broadcasted_iota(I32, shape, axis)


def out_kind(*shapes):
    return tuple(pltpu.VMEM(s, F32) for s in shapes)


def kernel(
    cfg,
    frontal,
    piece,
    lf_h1,
    lf_h,
    lo_h,
    sk_h,
    samples_out,
    interp_out,
    worst_out,
    a_v,
    pt,
    lf_s,
    lf_v,
    lo_v,
    sk_v,
    part,
    cx,
    s1,
    ph1,
    rot,
    pk,
    rx,
    table_v,
    table_s,
    w0,
    w1,
    w2,
    w3,
    a_sem,
    l_sem,
    t_sem,
    near_sem,
    pc_send,
    pc_recv,
    cx_send,
    cx_recv,
    p1_send,
    p1_recv,
    o_send,
    o_recv,
    m_send,
    m_recv,
):
    (rows, width, p_all, ny, nx, leaves_group, skel, cap, chunk) = cfg
    n_chunk = rows // chunk
    per_run = chunk // RUN
    half = n_chunk // 2
    tiles = rows // LANES
    half_p = p_all // 2
    sl = half_p // nx
    owners = 2 * nx
    n_col = owners * nx
    per_owner = cap // UNIT
    depth = width // ny

    g = lax.axis_index("row")
    me = lax.axis_index("col")
    core = lax.rem(me, 2)
    z = lax.rem(me // 2, nx)
    x = me // (2 * nx)
    q = jnp.where(core == 0, x, z)
    j_x = x * 2 + core
    me_next = x * 2 * nx + z * 2 + 1 - core

    def col_of(xx, zz, cc):
        return (xx * nx + zz) * 2 + cc

    def ring_a(pos):
        return col_of(jnp.where(core == 0, pos, x), jnp.where(core == 0, z, pos), core)

    def remote(src, dst, send_at, recv_at, row, col):
        return pltpu.make_async_remote_copy(
            src_ref=src,
            dst_ref=dst,
            send_sem=send_at,
            recv_sem=recv_at,
            device_id=(row, col),
            device_id_type=MESH,
        )

    def signal(sem, row, col):
        pl.semaphore_signal(sem, inc=1, device_id=(row, col), device_id_type=MESH)

    barrier = pltpu.get_barrier_semaphore()
    count = 0
    for d in range(1, ny):
        signal(barrier, lax.rem(g + d, ny), me)
        count += 1
    for d in range(1, owners):
        j = lax.rem(j_x + d, owners)
        signal(barrier, g, col_of(j // 2, z, lax.rem(j, 2)))
        count += 1
    for d in range(1, nx):
        for cc in range(2):
            signal(barrier, g, col_of(x, lax.rem(z + d, nx), cc))
            count += 1

    def load(i):
        at = pl.ds(pl.multiple_of(i * chunk, chunk), chunk)
        return pltpu.make_async_copy(frontal.at[at], a_v.at[at], a_sem.at[i])

    own_at = pl.ds(pl.multiple_of(g * depth, LANES), depth)
    small = [
        pltpu.make_async_copy(piece, pt.at[:, own_at], l_sem.at[0]),
        pltpu.make_async_copy(lf_h1, lf_s, l_sem.at[1]),
        pltpu.make_async_copy(lf_h, lf_v, l_sem.at[2]),
        pltpu.make_async_copy(lo_h, lo_v, l_sem.at[3]),
        pltpu.make_async_copy(sk_h, sk_v, l_sem.at[4]),
    ]
    for c in small:
        c.start()
    for i in range(n_chunk):
        load(i).start()
    small[0].wait()
    pl.semaphore_wait(barrier, count)

    drains = []

    def piece_copy(d):
        to = lax.rem(g + d, ny)
        return remote(pt.at[:, own_at], pt.at[:, own_at], pc_send, pc_recv.at[d - 1], to, me)

    def piece_sends():
        at = pl.ds(0, (ny - 1) * depth)
        remote(pt.at[:, at], pt.at[:, at], pc_send, pc_recv.at[0], g, me_next).wait_send()

    turns = sorted(range(1, ny), key=lambda d: min(d, ny - d))
    for d in turns:
        piece_copy(d).start()
    drains.append(piece_sends)

    for d in range(1, nx):
        signal(near_sem, g, col_of(x, lax.rem(z + d, nx), core))
    for d in range(1, ny):
        signal(near_sem, lax.rem(g + d, ny), me)

    small[1].wait()

    def mask_run(t):
        run = g * (rows // RUN) + t
        blocks = width // RUN

        @pl.when(run // blocks == me)
        def _():
            r0 = pl.multiple_of(t * RUN, RUN)
            c0 = pl.multiple_of(lax.rem(run, blocks) * RUN, RUN)
            ri = iota((RUN, RUN), 0) + run * RUN
            ci = iota((RUN, RUN), 1) + run * RUN
            rl = jnp.zeros((RUN, RUN), I32)
            cl = jnp.zeros((RUN, RUN), I32)
            for k in range(1, 4):
                edge = lf_s[run * 4 + k]
                rl = rl + jnp.where(ri >= edge, 1, 0)
                cl = cl + jnp.where(ci >= edge, 1, 0)
            block = a_v[pl.ds(r0, RUN), pl.ds(c0, RUN)].astype(F32)
            a_v[pl.ds(r0, RUN), pl.ds(c0, RUN)] = jnp.where(rl == cl, 0.0, block).astype(jnp.bfloat16)

    def product(at, d):
        k_at = pl.ds(pl.multiple_of(lax.rem(g + d, ny) * depth, LANES), depth)
        return dot(pt[:, k_at], a_v[at, k_at], NT)

    for h in range(2):
        for i in range(h * half, (h + 1) * half):
            load(i).wait()
        for t in range(h * half * per_run, (h + 1) * half * per_run):
            mask_run(t)
        at = pl.ds(h * half * chunk, half * chunk)
        part[:, at] = product(at, 0)

    sibling = col_of(x, z, 1 - core)

    def core_copy(i):
        at = pl.ds(pl.multiple_of(i * chunk, chunk), chunk)
        theirs = pl.ds(pl.multiple_of((1 - core) * half_p, half_p), half_p)
        return remote(part.at[theirs, at], cx.at[:, at], cx_send, cx_recv.at[i], g, sibling)

    def first_copy(i, d):
        to = lax.rem(q + d, nx)
        at = pl.ds(pl.multiple_of(i * chunk, chunk), chunk)
        rows_at = pl.ds(pl.multiple_of(to * sl, sl), sl)
        return remote(s1.at[rows_at, at], ph1.at[d - 1, :, at], p1_send, p1_recv.at[i], g, ring_a(to))

    def core_sum(i):
        at = pl.ds(pl.multiple_of(i * chunk, chunk), chunk)
        own = pl.ds(pl.multiple_of(core * half_p, half_p), half_p)
        core_copy(i).wait_recv()
        s1[:, at] = part[own, at] + cx[:, at]
        for d in sorted(range(1, nx), key=lambda d: -min(d, nx - d)):
            first_copy(i, d).start()

    piece_copy(turns[0]).wait_recv()
    part[...] += product(pl.ds(0, rows), ny - turns[0])
    for d in turns[1:]:
        piece_copy(d).wait_recv()
    lag = 2
    for i in range(n_chunk + lag):
        if i < n_chunk:
            at = pl.ds(i * chunk, chunk)
            v = part[:, at]
            for d in turns[1:]:
                v = v + product(at, ny - d)
            part[:, at] = v
            core_copy(i).start()
        if i >= lag:
            core_sum(i - lag)
    drains.append(lambda: remote(cx, cx, cx_send, cx_recv.at[0], g, sibling).wait_send())
    drains.append(lambda: remote(ph1, ph1, p1_send, p1_recv.at[0], g, sibling).wait_send())

    for c in small[2:]:
        c.wait()
    nl = leaves_group
    lane = iota((1, LANES), 1)

    def group_lanes(v):
        out = None
        for gi in range(ny):
            part_v = v if gi == 0 else pltpu.roll(v, v.shape[1] - gi * nl, axis=1)
            part_v = part_v[:, :LANES]
            out = part_v if out is None else jnp.where(g == gi, part_v, out)
        return out

    first = group_lanes(lf_v[...])
    owner = group_lanes(lo_v[...])
    real = lane < nl
    owner = jnp.where(real, owner, -1)
    fu = jnp.where(real, (first - g * rows) // UNIT, 0)
    nxt = pltpu.roll(fu, LANES - 1, axis=1)
    nxt = jnp.where(lane == nl - 1, rows // UNIT, nxt)
    su = jnp.where(real, nxt - fu, 0)
    owner_t = jnp.transpose(jnp.broadcast_to(owner, (LANES, LANES)))
    fu_t = jnp.transpose(jnp.broadcast_to(fu, (LANES, LANES)))
    su_t = jnp.transpose(jnp.broadcast_to(su, (LANES, LANES)))
    li = iota((LANES, LANES), 0)
    lj = iota((LANES, LANES), 1)
    same = owner == owner_t
    before = same & (li < lj)
    after = same & (lj < li)
    off = jnp.sum(jnp.where(before, su_t, 0), axis=0, keepdims=True)
    rank = jnp.sum(jnp.where(before, 1, 0), axis=0, keepdims=True)
    off_t = jnp.sum(jnp.where(after, su, 0), axis=1, keepdims=True)
    rank_t = jnp.sum(jnp.where(after, 1, 0), axis=1, keepdims=True)
    dst = iota((1, n_col * per_owner), 1)
    d_owner = dst // per_owner
    d_su = lax.rem(dst, per_owner)
    o1 = owner_t[:, :1]
    f1 = fu_t[:, :1]
    u1 = su_t[:, :1]
    hit = (o1 == d_owner) & (off_t <= d_su) & (d_su < off_t + u1)
    src = jnp.sum(jnp.where(hit, f1 + d_su - off_t + 1, 0), axis=0, keepdims=True) - 1
    per_tile = LANES // UNIT
    turn = lax.rem(d_su - src + 8 * per_tile * rows, per_tile)
    entry = jnp.where(src >= 0, turn * tiles + src // per_tile, per_tile * tiles)
    table_v[...] = entry
    to_smem = pltpu.make_async_copy(table_v, table_s, t_sem)
    to_smem.start()

    slot = iota((1, cap), 1)
    slot_u = slot // UNIT
    mine_t = (o1 == me) & (off_t <= slot_u) & (slot_u < off_t + u1)
    slot_rank = jnp.sum(jnp.where(mine_t, rank_t + 1, 0), axis=0, keepdims=True) - 1
    sk = group_lanes(sk_v[...])
    sk_slot = sk - first + off * UNIT + 1
    cols = []
    for k in range(LEAF_MOST):
        pick_k = (owner == me) & (rank == k)
        cols.append(jnp.sum(jnp.where(pick_k, sk_slot, 0), axis=1, keepdims=True))
    sk_col = jnp.concatenate(cols, axis=0)
    hot = jnp.where(sk_col == slot + 1, 1.0, 0.0).astype(F32)
    ki = LEAF_MOST * skel
    row_k = iota((ki, 1), 0) // skel

    rot[per_tile * tiles] = jnp.zeros((sl, LANES), F32)

    def first_sum(i, carry):
        every = ph1.at[:, :, pl.ds(pl.multiple_of(i * chunk, chunk), chunk)]
        remote(every, every, p1_send, p1_recv.at[i], g, sibling).wait_recv()
        own = pl.ds(pl.multiple_of(q * sl, sl), sl)
        for t in range(chunk // LANES):
            at = pl.ds(pl.multiple_of(i * chunk + t * LANES, LANES), LANES)
            v = s1[own, at]
            for d in range(1, nx):
                v = v + ph1[d - 1, :, at]
            tile = i * (chunk // LANES) + t
            rot[tile] = v
            for k in range(1, per_tile):
                rot[k * tiles + tile] = pltpu.roll(v, k * UNIT, axis=1)
        return carry

    lax.fori_loop(0, n_chunk, first_sum, 0)

    to_smem.wait()
    pl.semaphore_wait(near_sem, nx - 1 + ny - 1)
    lane_u = iota((sl, LANES), 1) // UNIT

    def there(k):
        dx, dz, dc = k
        return col_of(lax.rem(x + dx, nx), lax.rem(z + dz, nx), lax.rem(core + dc, 2))

    def owner_copy(n, k):
        return remote(pk.at[n], rx.at[me], o_send, o_recv, g, there(k))

    def block_of(o, h):
        base = o * per_owner + h * per_tile
        v = rot[table_s[0, base]]
        for k in range(1, per_tile):
            v = jnp.where(lane_u == k, rot[table_s[0, base + k]], v)
        return v

    steps = [(dx, dz, dc) for dx in range(nx) for dz in range(nx) for dc in range(2)]
    steps.sort(key=lambda k: -(min(k[0], nx - k[0]) + min(k[1], nx - k[1])))
    steps = [k for k in steps if k != (0, 0, 0)]
    for n, k in enumerate(steps):
        o = there(k)
        for h in range(cap // LANES):
            pk[n, :, h * LANES : (h + 1) * LANES] = block_of(o, h)
        owner_copy(n, k).start()
    for h in range(cap // LANES):
        rx[me, :, h * LANES : (h + 1) * LANES] = block_of(me, h)
    blocks_in = remote(pk, rx.at[: n_col - 1], o_send, o_recv, g, sibling)
    blocks_in.wait_recv()
    drains.append(blocks_in.wait_send)

    def total(ids):
        v = rx[ids[0]]
        for s in ids[1:]:
            v = v + rx[s]
        return v

    m = jnp.concatenate(
        [total([col_of(a, b, 0) for b in range(nx)]) for a in range(nx)]
        + [total([col_of(b, a, 1) for b in range(nx)]) for a in range(nx)],
        axis=0,
    )

    samples_out[...] = m
    pick = dot(hot, m, NT, HI)
    pick_t = dot(m, hot, NT, HI)
    rhs = dot(pick, m, NN, HI)
    gram = dot(pick, pick, NT, HI)
    col_k = iota((1, ki), 1) // skel
    in_block = row_k == col_k
    gram = jnp.where(in_block, gram, 0.0)
    folded = gram[:skel]
    for k in range(1, LEAF_MOST):
        folded = folded + gram[k * skel : (k + 1) * skel]
    here = jnp.concatenate(
        [jnp.broadcast_to(jnp.where(c[:1] > 0, 1, 0), (1, skel)) for c in cols], axis=1
    )
    eye_i = iota((skel, ki), 0)
    eye_r = lax.rem(iota((skel, ki), 1), skel)
    a = []
    for j in range(skel):
        v = None
        for k in range(LEAF_MOST):
            c = jnp.broadcast_to(folded[:, k * skel + j : k * skel + j + 1], (skel, ki))
            v = c if v is None else jnp.where(col_k == k, c, v)
        a.append(v + jnp.where((eye_i == j) & (here == 0), 1.0, 0.0))
    inv = jnp.where(eye_i == eye_r, 1.0, 0.0).astype(F32)
    for s in range(skel):
        col = a[s]
        rcp = 1.0 / col[s : s + 1]
        at_s = eye_i == s
        for j in range(s + 1, skel):
            t = a[j][s : s + 1] * rcp
            a[j] = jnp.where(at_s, t, a[j] - col * t)
        t = inv[s : s + 1] * rcp
        inv = jnp.where(at_s, t, inv - col * t)
    inv_all = jnp.where(in_block, jnp.concatenate([inv] * LEAF_MOST, axis=0), 0.0)
    rhs = jnp.where(row_k == slot_rank, rhs, 0.0)
    coeff = dot(inv_all, rhs, NN, HI)
    resid = m - dot(pick_t, coeff, NN, HI)
    err = jnp.sum(resid * resid, axis=0, keepdims=True)
    norm = jnp.sum(m * m, axis=0, keepdims=True)
    of_k = iota((8, 1), 0) == slot_rank
    err = jnp.sum(jnp.where(of_k, err, 0.0), axis=1, keepdims=True)
    norm = jnp.sum(jnp.where(of_k, norm, 0.0), axis=1, keepdims=True)
    ratio = jnp.sqrt(err) / jnp.sqrt(norm + 1e-06)
    w0[...] = jnp.broadcast_to(jnp.max(ratio, axis=0, keepdims=True), w0.shape)

    def m1(d):
        j = lax.rem(j_x + d, owners)
        to = col_of(j // 2, z, lax.rem(j, 2))
        return remote(w0.at[:1], w1.at[d - 1, :1], m_send.at[0], m_recv.at[0], g, to)

    def m2(d):
        to_y = lax.rem(g + d // nx, ny)
        to = col_of(x, lax.rem(z + d % nx, nx), core)
        return remote(w2.at[:1], w3.at[d - 1, :1], m_send.at[1], m_recv.at[1], to_y, to)

    for d in sorted(range(1, owners), key=lambda d: -min(d, owners - d)):
        m1(d).start()
    folded_c = coeff[:skel]
    for k in range(1, LEAF_MOST):
        folded_c = folded_c + coeff[k * skel : (k + 1) * skel]
    interp_out[...] = folded_c
    all1 = remote(w1.at[:, :1], w1.at[:, :1], m_send.at[0], m_recv.at[0], g, sibling)
    all1.wait_recv()
    v = w0[:1]
    for d in range(1, owners):
        v = jnp.maximum(v, w1[d - 1, :1])
    w2[...] = jnp.broadcast_to(v, w2.shape)
    for d in sorted(range(1, nx * ny), key=lambda d: -min(d % nx, nx - d % nx) - min(d // nx, ny - d // nx)):
        m2(d).start()
    for f in drains:
        f()
    all1.wait_send()
    all2 = remote(w3.at[:, :1], w3.at[:, :1], m_send.at[1], m_recv.at[1], g, sibling)
    all2.wait_send()
    all2.wait_recv()
    for d in range(1, nx * ny):
        v = jnp.maximum(v, w3[d - 1, :1])
    worst_out[...] = v


def finish(a_ref, b_ref, c_ref, a_out, b_out, c_out):
    a_out[...] = a_ref[...]
    b_out[...] = b_ref[...]
    c_out[...] = c_ref[:, :1]


def local(frontal, sample_cols, leaf_first, leaf_owner, skeleton):
    rows, width = frontal.shape
    p_all = sample_cols.shape[1]
    leaves, skel = skeleton.shape
    n_col = lax.axis_size("col")
    ny = lax.axis_size("row")
    nx = math.isqrt(n_col // 2)
    cap = 2 * rows // n_col
    chunk = rows // 4
    n_chunk = rows // chunk
    tiles = rows // LANES
    half_p = p_all // 2
    sl = half_p // nx
    owners = 2 * nx
    cfg = (rows, width, p_all, ny, nx, leaves // ny, skel, cap, chunk)
    slots_all = n_col * cap // UNIT
    hbm = pl.BlockSpec(memory_space=pl.ANY)
    vmem = pl.BlockSpec(memory_space=pltpu.VMEM)
    dma = pltpu.SemaphoreType.DMA
    pad = ((0, 0), (0, max(0, LANES - leaves)))
    wide = leaves + pad[1][1]
    results = pl.pallas_call(
        functools.partial(kernel, cfg),
        out_shape=out_kind((p_all, cap), (skel, cap), (1, LANES)),
        in_specs=[hbm] * 6,
        out_specs=(vmem, vmem, vmem),
        scratch_shapes=[
            pltpu.VMEM((rows, width), jnp.bfloat16),
            pltpu.VMEM((p_all, width), jnp.bfloat16),
            pltpu.SMEM((leaves,), I32),
            pltpu.VMEM((1, wide), I32),
            pltpu.VMEM((1, wide), I32),
            pltpu.VMEM((skel, wide), I32),
            pltpu.VMEM((p_all, rows), F32),
            pltpu.VMEM((half_p, rows), F32),
            pltpu.VMEM((half_p, rows), F32),
            pltpu.VMEM((nx - 1, sl, rows), F32),
            pltpu.VMEM((4 * tiles + 1, sl, LANES), F32),
            pltpu.VMEM((n_col - 1, sl, cap), F32),
            pltpu.VMEM((n_col, sl, cap), F32),
            pltpu.VMEM((1, slots_all), I32),
            pltpu.SMEM((1, slots_all), I32),
            pltpu.VMEM((8, LANES), F32),
            pltpu.VMEM((owners - 1, 8, LANES), F32),
            pltpu.VMEM((8, LANES), F32),
            pltpu.VMEM((nx * ny - 1, 8, LANES), F32),
            dma((n_chunk,)),
            dma((5,)),
            dma(()),
            pltpu.SemaphoreType.REGULAR,
            dma(()),
            dma((ny - 1,)),
            dma(()),
            dma((n_chunk,)),
            dma(()),
            dma((n_chunk,)),
            dma(()),
            dma(()),
            dma((2,)),
            dma((2,)),
        ],
        compiler_params=pltpu.CompilerParams(
            collective_id=0, has_side_effects=True, vmem_limit_bytes=56 << 20
        ),
        name="round",
    )(
        frontal,
        sample_cols.T,
        leaf_first,
        jnp.pad(leaf_first.reshape(1, leaves), pad),
        jnp.pad(leaf_owner.reshape(1, leaves), pad),
        jnp.pad(skeleton.T, pad),
    )
    samples, interp, worst = pl.pallas_call(
        finish,
        out_shape=(
            jax.ShapeDtypeStruct((p_all, cap), F32),
            jax.ShapeDtypeStruct((skel, cap), F32),
            jax.ShapeDtypeStruct((1, 1), F32),
        ),
        in_specs=[vmem] * 3,
        out_specs=(vmem,) * 3,
        name="finish",
    )(*(pltpu.with_memory_space_constraint(r, pltpu.VMEM) for r in results))
    return samples, interp, worst.reshape(1)


def solution(mesh):
    return jax.shard_map(
        local,
        mesh=mesh,
        in_specs=(P("row", "col"), P(("col", "row"), None), P(), P(), P()),
        out_specs=(P("row", "col"), P("row", "col"), P()),
        check_vma=False,
    )
```

```python
import functools
import math

import jax
import jax.numpy as jnp
from jax import lax
from jax.experimental import pallas as pl
from jax.experimental.pallas import tpu as pltpu
from jax.sharding import PartitionSpec as P

UNIT = 32
RUN = 256
LANES = 128
LEAF_MOST = 4
F32 = jnp.float32
I32 = jnp.int32
MESH = pl.DeviceIdType.MESH
HI = lax.Precision.HIGHEST
NT = (((1,), (1,)), ((), ()))
NN = (((1,), (0,)), ((), ()))


def dot(a, b, dims, precision=None):
    return lax.dot_general(a, b, dims, precision=precision, preferred_element_type=F32)


def iota(shape, axis):
    return lax.broadcasted_iota(I32, shape, axis)


def out_kind(*shapes):
    return tuple(pltpu.VMEM(s, F32) for s in shapes)


def kernel(
    cfg,
    frontal,
    piece,
    lf_h1,
    lf_h,
    lo_h,
    sk_h,
    samples_out,
    interp_out,
    worst_out,
    a_v,
    pt,
    lf_s,
    lf_v,
    lo_v,
    sk_v,
    part,
    cx,
    s1,
    ph1,
    rot,
    pk,
    rx,
    table_v,
    table_s,
    w0,
    w1,
    w2,
    w3,
    a_sem,
    l_sem,
    t_sem,
    near_sem,
    pc_send,
    pc_recv,
    cx_send,
    cx_recv,
    p1_send,
    p1_recv,
    o_send,
    o_recv,
    m_send,
    m_recv,
):
    (rows, width, p_all, ny, nx, leaves_group, skel, cap, chunk) = cfg
    n_chunk = rows // chunk
    per_run = chunk // RUN
    half = n_chunk // 2
    tiles = rows // LANES
    half_p = p_all // 2
    sl = half_p // nx
    owners = 2 * nx
    n_col = owners * nx
    per_owner = cap // UNIT
    depth = width // ny

    g = lax.axis_index("row")
    me = lax.axis_index("col")
    core = lax.rem(me, 2)
    z = lax.rem(me // 2, nx)
    x = me // (2 * nx)
    q = jnp.where(core == 0, x, z)
    j_x = x * 2 + core
    me_next = x * 2 * nx + z * 2 + 1 - core

    def col_of(xx, zz, cc):
        return (xx * nx + zz) * 2 + cc

    def ring_a(pos):
        return col_of(jnp.where(core == 0, pos, x), jnp.where(core == 0, z, pos), core)

    def remote(src, dst, send_at, recv_at, row, col):
        return pltpu.make_async_remote_copy(
            src_ref=src,
            dst_ref=dst,
            send_sem=send_at,
            recv_sem=recv_at,
            device_id=(row, col),
            device_id_type=MESH,
        )

    def signal(sem, row, col):
        pl.semaphore_signal(sem, inc=1, device_id=(row, col), device_id_type=MESH)

    barrier = pltpu.get_barrier_semaphore()
    count = 0
    for d in range(1, ny):
        signal(barrier, lax.rem(g + d, ny), me)
        count += 1
    for d in range(1, owners):
        j = lax.rem(j_x + d, owners)
        signal(barrier, g, col_of(j // 2, z, lax.rem(j, 2)))
        count += 1
    for d in range(1, nx):
        for cc in range(2):
            signal(barrier, g, col_of(x, lax.rem(z + d, nx), cc))
            count += 1

    def load(i):
        at = pl.ds(pl.multiple_of(i * chunk, chunk), chunk)
        return pltpu.make_async_copy(frontal.at[at], a_v.at[at], a_sem.at[i])

    own_at = pl.ds(pl.multiple_of(g * depth, LANES), depth)
    small = [
        pltpu.make_async_copy(piece, pt.at[:, own_at], l_sem.at[0]),
        pltpu.make_async_copy(lf_h1, lf_s, l_sem.at[1]),
        pltpu.make_async_copy(lf_h, lf_v, l_sem.at[2]),
        pltpu.make_async_copy(lo_h, lo_v, l_sem.at[3]),
        pltpu.make_async_copy(sk_h, sk_v, l_sem.at[4]),
    ]
    for c in small:
        c.start()
    for i in range(n_chunk):
        load(i).start()
    small[0].wait()
    pl.semaphore_wait(barrier, count)

    drains = []

    def piece_copy(d):
        to = lax.rem(g + d, ny)
        return remote(pt.at[:, own_at], pt.at[:, own_at], pc_send, pc_recv.at[d - 1], to, me)

    def piece_sends():
        at = pl.ds(0, (ny - 1) * depth)
        remote(pt.at[:, at], pt.at[:, at], pc_send, pc_recv.at[0], g, me_next).wait_send()

    turns = sorted(range(1, ny), key=lambda d: min(d, ny - d))
    for d in turns:
        piece_copy(d).start()
    drains.append(piece_sends)

    for d in range(1, nx):
        signal(near_sem, g, col_of(x, lax.rem(z + d, nx), core))
    for d in range(1, ny):
        signal(near_sem, lax.rem(g + d, ny), me)

    small[1].wait()

    def mask_run(t):
        run = g * (rows // RUN) + t
        blocks = width // RUN

        @pl.when(run // blocks == me)
        def _():
            r0 = pl.multiple_of(t * RUN, RUN)
            c0 = pl.multiple_of(lax.rem(run, blocks) * RUN, RUN)
            ri = iota((RUN, RUN), 0) + run * RUN
            ci = iota((RUN, RUN), 1) + run * RUN
            rl = jnp.zeros((RUN, RUN), I32)
            cl = jnp.zeros((RUN, RUN), I32)
            for k in range(1, 4):
                edge = lf_s[run * 4 + k]
                rl = rl + jnp.where(ri >= edge, 1, 0)
                cl = cl + jnp.where(ci >= edge, 1, 0)
            block = a_v[pl.ds(r0, RUN), pl.ds(c0, RUN)].astype(F32)
            a_v[pl.ds(r0, RUN), pl.ds(c0, RUN)] = jnp.where(rl == cl, 0.0, block).astype(jnp.bfloat16)

    def product(at, d):
        k_at = pl.ds(pl.multiple_of(lax.rem(g + d, ny) * depth, LANES), depth)
        return dot(pt[:, k_at], a_v[at, k_at], NT)

    for h in range(2):
        for i in range(h * half, (h + 1) * half):
            load(i).wait()
        for t in range(h * half * per_run, (h + 1) * half * per_run):
            mask_run(t)
        at = pl.ds(h * half * chunk, half * chunk)
        part[:, at] = product(at, 0)

    sibling = col_of(x, z, 1 - core)

    def core_copy(i):
        at = pl.ds(pl.multiple_of(i * chunk, chunk), chunk)
        theirs = pl.ds(pl.multiple_of((1 - core) * half_p, half_p), half_p)
        return remote(part.at[theirs, at], cx.at[:, at], cx_send, cx_recv.at[i], g, sibling)

    def first_copy(i, d):
        to = lax.rem(q + d, nx)
        at = pl.ds(pl.multiple_of(i * chunk, chunk), chunk)
        rows_at = pl.ds(pl.multiple_of(to * sl, sl), sl)
        return remote(s1.at[rows_at, at], ph1.at[d - 1, :, at], p1_send, p1_recv.at[i], g, ring_a(to))

    def core_sum(i):
        at = pl.ds(pl.multiple_of(i * chunk, chunk), chunk)
        own = pl.ds(pl.multiple_of(core * half_p, half_p), half_p)
        core_copy(i).wait_recv()
        s1[:, at] = part[own, at] + cx[:, at]
        for d in sorted(range(1, nx), key=lambda d: -min(d, nx - d)):
            first_copy(i, d).start()

    piece_copy(turns[0]).wait_recv()
    part[...] += product(pl.ds(0, rows), ny - turns[0])
    for d in turns[1:]:
        piece_copy(d).wait_recv()
    lag = 2
    for i in range(n_chunk + lag):
        if i < n_chunk:
            at = pl.ds(i * chunk, chunk)
            v = part[:, at]
            for d in turns[1:]:
                v = v + product(at, ny - d)
            part[:, at] = v
            core_copy(i).start()
        if i >= lag:
            core_sum(i - lag)
    drains.append(lambda: remote(cx, cx, cx_send, cx_recv.at[0], g, sibling).wait_send())
    drains.append(lambda: remote(ph1, ph1, p1_send, p1_recv.at[0], g, sibling).wait_send())

    for c in small[2:]:
        c.wait()
    nl = leaves_group
    lane = iota((1, LANES), 1)

    def group_lanes(v):
        out = None
        for gi in range(ny):
            part_v = v if gi == 0 else pltpu.roll(v, v.shape[1] - gi * nl, axis=1)
            part_v = part_v[:, :LANES]
            out = part_v if out is None else jnp.where(g == gi, part_v, out)
        return out

    first = group_lanes(lf_v[...])
    owner = group_lanes(lo_v[...])
    real = lane < nl
    owner = jnp.where(real, owner, -1)
    fu = jnp.where(real, (first - g * rows) // UNIT, 0)
    nxt = pltpu.roll(fu, LANES - 1, axis=1)
    nxt = jnp.where(lane == nl - 1, rows // UNIT, nxt)
    su = jnp.where(real, nxt - fu, 0)
    owner_t = jnp.transpose(jnp.broadcast_to(owner, (LANES, LANES)))
    fu_t = jnp.transpose(jnp.broadcast_to(fu, (LANES, LANES)))
    su_t = jnp.transpose(jnp.broadcast_to(su, (LANES, LANES)))
    li = iota((LANES, LANES), 0)
    lj = iota((LANES, LANES), 1)
    same = owner == owner_t
    before = same & (li < lj)
    after = same & (lj < li)
    off = jnp.sum(jnp.where(before, su_t, 0), axis=0, keepdims=True)
    rank = jnp.sum(jnp.where(before, 1, 0), axis=0, keepdims=True)
    off_t = jnp.sum(jnp.where(after, su, 0), axis=1, keepdims=True)
    rank_t = jnp.sum(jnp.where(after, 1, 0), axis=1, keepdims=True)
    dst = iota((1, n_col * per_owner), 1)
    d_owner = dst // per_owner
    d_su = lax.rem(dst, per_owner)
    o1 = owner_t[:, :1]
    f1 = fu_t[:, :1]
    u1 = su_t[:, :1]
    hit = (o1 == d_owner) & (off_t <= d_su) & (d_su < off_t + u1)
    src = jnp.sum(jnp.where(hit, f1 + d_su - off_t + 1, 0), axis=0, keepdims=True) - 1
    per_tile = LANES // UNIT
    turn = lax.rem(d_su - src + 8 * per_tile * rows, per_tile)
    entry = jnp.where(src >= 0, turn * tiles + src // per_tile, per_tile * tiles)
    table_v[...] = entry
    to_smem = pltpu.make_async_copy(table_v, table_s, t_sem)
    to_smem.start()

    slot = iota((1, cap), 1)
    slot_u = slot // UNIT
    mine_t = (o1 == me) & (off_t <= slot_u) & (slot_u < off_t + u1)
    slot_rank = jnp.sum(jnp.where(mine_t, rank_t + 1, 0), axis=0, keepdims=True) - 1
    sk = group_lanes(sk_v[...])
    sk_slot = sk - first + off * UNIT + 1
    cols = []
    for k in range(LEAF_MOST):
        pick_k = (owner == me) & (rank == k)
        cols.append(jnp.sum(jnp.where(pick_k, sk_slot, 0), axis=1, keepdims=True))
    sk_col = jnp.concatenate(cols, axis=0)
    hot = jnp.where(sk_col == slot + 1, 1.0, 0.0).astype(F32)
    ki = LEAF_MOST * skel
    row_k = iota((ki, 1), 0) // skel

    rot[per_tile * tiles] = jnp.zeros((sl, LANES), F32)

    def first_sum(i, carry):
        every = ph1.at[:, :, pl.ds(pl.multiple_of(i * chunk, chunk), chunk)]
        remote(every, every, p1_send, p1_recv.at[i], g, sibling).wait_recv()
        own = pl.ds(pl.multiple_of(q * sl, sl), sl)
        for t in range(chunk // LANES):
            at = pl.ds(pl.multiple_of(i * chunk + t * LANES, LANES), LANES)
            v = s1[own, at]
            for d in range(1, nx):
                v = v + ph1[d - 1, :, at]
            tile = i * (chunk // LANES) + t
            rot[tile] = v
            for k in range(1, per_tile):
                rot[k * tiles + tile] = pltpu.roll(v, k * UNIT, axis=1)
        return carry

    lax.fori_loop(0, n_chunk, first_sum, 0)

    to_smem.wait()
    pl.semaphore_wait(near_sem, nx - 1 + ny - 1)
    lane_u = iota((sl, LANES), 1) // UNIT

    def there(k):
        dx, dz, dc = k
        return col_of(lax.rem(x + dx, nx), lax.rem(z + dz, nx), lax.rem(core + dc, 2))

    def owner_copy(n, k):
        return remote(pk.at[n], rx.at[me], o_send, o_recv, g, there(k))

    def block_of(o, h):
        base = o * per_owner + h * per_tile
        v = rot[table_s[0, base]]
        for k in range(1, per_tile):
            v = jnp.where(lane_u == k, rot[table_s[0, base + k]], v)
        return v

    steps = [(dx, dz, dc) for dx in range(nx) for dz in range(nx) for dc in range(2)]
    turn_of = {n: m for m, n in enumerate([1, nx - 1, *range(2, nx - 1), 0])}
    steps.sort(
        key=lambda k: (
            -(min(k[0], nx - k[0]) + min(k[1], nx - k[1])),
            k[2],
            turn_of[k[1]],
            turn_of[k[0]],
        )
    )
    steps = [k for k in steps if k != (0, 0, 0)]
    for n, k in enumerate(steps):
        o = there(k)
        for h in range(cap // LANES):
            pk[n, :, h * LANES : (h + 1) * LANES] = block_of(o, h)
        owner_copy(n, k).start()
    for h in range(cap // LANES):
        rx[me, :, h * LANES : (h + 1) * LANES] = block_of(me, h)
    blocks_in = remote(pk, rx.at[: n_col - 1], o_send, o_recv, g, sibling)
    blocks_in.wait_recv()
    drains.append(blocks_in.wait_send)

    def total(ids):
        v = rx[ids[0]]
        for s in ids[1:]:
            v = v + rx[s]
        return v

    m = jnp.concatenate(
        [total([col_of(a, b, 0) for b in range(nx)]) for a in range(nx)]
        + [total([col_of(b, a, 1) for b in range(nx)]) for a in range(nx)],
        axis=0,
    )

    samples_out[...] = m
    terms = []
    rest = m
    for _ in range(3):
        terms.append(rest.astype(jnp.bfloat16))
        rest = rest - terms[-1].astype(F32)
    hot16 = hot.astype(jnp.bfloat16)
    pick = sum(dot(hot16, t, NT) for t in terms)
    pick_t = sum(dot(t, hot16, NT) for t in terms)
    rhs = dot(pick, m, NN, HI)
    gram = dot(pick, pick, NT, HI)
    col_k = iota((1, ki), 1) // skel
    in_block = row_k == col_k
    gram = jnp.where(in_block, gram, 0.0)
    folded = gram[:skel]
    for k in range(1, LEAF_MOST):
        folded = folded + gram[k * skel : (k + 1) * skel]
    here = jnp.concatenate(
        [jnp.broadcast_to(jnp.where(c[:1] > 0, 1, 0), (1, skel)) for c in cols], axis=1
    )
    eye_i = iota((skel, ki), 0)
    eye_r = lax.rem(iota((skel, ki), 1), skel)
    a = []
    for j in range(skel):
        v = None
        for k in range(LEAF_MOST):
            c = jnp.broadcast_to(folded[:, k * skel + j : k * skel + j + 1], (skel, ki))
            v = c if v is None else jnp.where(col_k == k, c, v)
        a.append(v + jnp.where((eye_i == j) & (here == 0), 1.0, 0.0))
    inv = jnp.where(eye_i == eye_r, 1.0, 0.0).astype(F32)
    for s in range(skel):
        col = a[s]
        rcp = 1.0 / col[s : s + 1]
        at_s = eye_i == s
        for j in range(s + 1, skel):
            t = a[j][s : s + 1] * rcp
            a[j] = jnp.where(at_s, t, a[j] - col * t)
        t = inv[s : s + 1] * rcp
        inv = jnp.where(at_s, t, inv - col * t)
    inv_all = jnp.where(in_block, jnp.concatenate([inv] * LEAF_MOST, axis=0), 0.0)
    rhs = jnp.where(row_k == slot_rank, rhs, 0.0)
    coeff = dot(inv_all, rhs, NN, HI)
    resid = m - dot(pick_t, coeff, NN, HI)
    err = jnp.sum(resid * resid, axis=0, keepdims=True)
    norm = jnp.sum(m * m, axis=0, keepdims=True)
    of_k = iota((8, 1), 0) == slot_rank
    err = jnp.sum(jnp.where(of_k, err, 0.0), axis=1, keepdims=True)
    norm = jnp.sum(jnp.where(of_k, norm, 0.0), axis=1, keepdims=True)
    ratio = jnp.sqrt(err) / jnp.sqrt(norm + 1e-06)
    w0[...] = jnp.broadcast_to(jnp.max(ratio, axis=0, keepdims=True), w0.shape)

    def m1(d):
        j = lax.rem(j_x + d, owners)
        to = col_of(j // 2, z, lax.rem(j, 2))
        return remote(w0.at[:1], w1.at[d - 1, :1], m_send.at[0], m_recv.at[0], g, to)

    def m2(d):
        to_y = lax.rem(g + d // nx, ny)
        to = col_of(x, lax.rem(z + d % nx, nx), core)
        return remote(w2.at[:1], w3.at[d - 1, :1], m_send.at[1], m_recv.at[1], to_y, to)

    for d in sorted(range(1, owners), key=lambda d: -min(d, owners - d)):
        m1(d).start()
    folded_c = coeff[:skel]
    for k in range(1, LEAF_MOST):
        folded_c = folded_c + coeff[k * skel : (k + 1) * skel]
    interp_out[...] = folded_c
    all1 = remote(w1.at[:, :1], w1.at[:, :1], m_send.at[0], m_recv.at[0], g, sibling)
    all1.wait_recv()
    v = w0[:1]
    for d in range(1, owners):
        v = jnp.maximum(v, w1[d - 1, :1])
    w2[...] = jnp.broadcast_to(v, w2.shape)
    for d in sorted(range(1, nx * ny), key=lambda d: -min(d % nx, nx - d % nx) - min(d // nx, ny - d // nx)):
        m2(d).start()
    for f in drains:
        f()
    all1.wait_send()
    all2 = remote(w3.at[:, :1], w3.at[:, :1], m_send.at[1], m_recv.at[1], g, sibling)
    all2.wait_send()
    all2.wait_recv()
    for d in range(1, nx * ny):
        v = jnp.maximum(v, w3[d - 1, :1])
    worst_out[...] = v


def finish(a_ref, b_ref, c_ref, a_out, b_out, c_out):
    a_out[...] = a_ref[...]
    b_out[...] = b_ref[...]
    c_out[...] = c_ref[:, :1]


def local(frontal, sample_cols, leaf_first, leaf_owner, skeleton):
    rows, width = frontal.shape
    p_all = sample_cols.shape[1]
    leaves, skel = skeleton.shape
    n_col = lax.axis_size("col")
    ny = lax.axis_size("row")
    nx = math.isqrt(n_col // 2)
    cap = 2 * rows // n_col
    chunk = rows // 4
    n_chunk = rows // chunk
    tiles = rows // LANES
    half_p = p_all // 2
    sl = half_p // nx
    owners = 2 * nx
    cfg = (rows, width, p_all, ny, nx, leaves // ny, skel, cap, chunk)
    slots_all = n_col * cap // UNIT
    hbm = pl.BlockSpec(memory_space=pl.ANY)
    vmem = pl.BlockSpec(memory_space=pltpu.VMEM)
    dma = pltpu.SemaphoreType.DMA
    pad = ((0, 0), (0, max(0, LANES - leaves)))
    wide = leaves + pad[1][1]
    results = pl.pallas_call(
        functools.partial(kernel, cfg),
        out_shape=out_kind((p_all, cap), (skel, cap), (1, LANES)),
        in_specs=[hbm] * 6,
        out_specs=(vmem, vmem, vmem),
        scratch_shapes=[
            pltpu.VMEM((rows, width), jnp.bfloat16),
            pltpu.VMEM((p_all, width), jnp.bfloat16),
            pltpu.SMEM((leaves,), I32),
            pltpu.VMEM((1, wide), I32),
            pltpu.VMEM((1, wide), I32),
            pltpu.VMEM((skel, wide), I32),
            pltpu.VMEM((p_all, rows), F32),
            pltpu.VMEM((half_p, rows), F32),
            pltpu.VMEM((half_p, rows), F32),
            pltpu.VMEM((nx - 1, sl, rows), F32),
            pltpu.VMEM((4 * tiles + 1, sl, LANES), F32),
            pltpu.VMEM((n_col - 1, sl, cap), F32),
            pltpu.VMEM((n_col, sl, cap), F32),
            pltpu.VMEM((1, slots_all), I32),
            pltpu.SMEM((1, slots_all), I32),
            pltpu.VMEM((8, LANES), F32),
            pltpu.VMEM((owners - 1, 8, LANES), F32),
            pltpu.VMEM((8, LANES), F32),
            pltpu.VMEM((nx * ny - 1, 8, LANES), F32),
            dma((n_chunk,)),
            dma((5,)),
            dma(()),
            pltpu.SemaphoreType.REGULAR,
            dma(()),
            dma((ny - 1,)),
            dma(()),
            dma((n_chunk,)),
            dma(()),
            dma((n_chunk,)),
            dma(()),
            dma(()),
            dma((2,)),
            dma((2,)),
        ],
        compiler_params=pltpu.CompilerParams(
            collective_id=0, has_side_effects=True, vmem_limit_bytes=56 << 20
        ),
        name="round",
    )(
        frontal,
        sample_cols.T,
        leaf_first,
        jnp.pad(leaf_first.reshape(1, leaves), pad),
        jnp.pad(leaf_owner.reshape(1, leaves), pad),
        jnp.pad(skeleton.T, pad),
    )
    samples, interp, worst = pl.pallas_call(
        finish,
        out_shape=(
            jax.ShapeDtypeStruct((p_all, cap), F32),
            jax.ShapeDtypeStruct((skel, cap), F32),
            jax.ShapeDtypeStruct((1, 1), F32),
        ),
        in_specs=[vmem] * 3,
        out_specs=(vmem,) * 3,
        name="finish",
    )(*(pltpu.with_memory_space_constraint(r, pltpu.VMEM) for r in results))
    return samples, interp, worst.reshape(1)


def solution(mesh):
    return jax.shard_map(
        local,
        mesh=mesh,
        in_specs=(P("row", "col"), P(("col", "row"), None), P(), P(), P()),
        out_specs=(P("row", "col"), P("row", "col"), P()),
        check_vma=False,
    )
```
